128 devices in a mesh: cells: 32 (over z, x, core), rcpt: 4 (over y).
Axes of the slice: x: 4, y: 4, z: 4, core: 2. Of those that a mesh axis runs over, the one named last changes fastest.
Arguments:
- control: float32 [24, 256], replicated, may hold values from -3 to 3
- background: float32 [24, 524288], P(None, 'cells'), may hold values from 0.3 to 3
- ensemble: bfloat16 [256, 524288], P(None, 'cells'), may hold values from -0.3125 to 0.3125
- footprint: bfloat16 [4, 8192, 128, 128], P('rcpt', 'cells'), may hold values from 0.00023365021 to 0.0234375
- tile_block: int32 [4, 8192], P('rcpt', 'cells'), may hold values from 0 to 127
- tile_row: int32 [4, 8192], P('rcpt', 'cells'), may hold values from 0 to 2047, as said below
- tile_count: int32 [4, 32], P('rcpt', 'cells'), may hold values from 32 to 256, as said below
- hour: int32 [4, 262144], P('rcpt'), may hold values from 0 to 23
- observed: float32 [4, 262144], P('rcpt'), may hold values from -6 to 6
- inv_var: float32 [4, 262144], P('rcpt'), may hold values from 0.5 to 4
Outputs:
- gradients: float32 [2, 24, 256], replicated
- modelled_final: float32 [4, 262144], P('rcpt', 'cells')
The draws below stay inside these ranges and needn't reach their ends.
Inputs may be any that keep to these rules, and one draw needn't show every extreme that they name: `tile_count`: in every group one device holds exactly 256 live slots. Slots at or past a device's count hold no tile and are ignored. `tile_row`: receptor tiles fall into 32 shares of 64 consecutive tiles. Of the 256 slots of one device (slots c * 256 to (c + 1) * 256 - 1 of a group), exactly 8 name tiles of each share.
All inputs are finite; a program needn't handle non-finite values.
Results may differ from the reference program's by a relative error of at most 0.0059.
Values may be sent and summed in bfloat16 or wider, within the bound.
No kernel may reach another device: no remote copies, remote signals or barrier semaphores. Data moves between devices by JAX's collectives and lax.ppermute only.
A program may use at most 128 MiB of HBM per device.

```python
import math
import jax
import jax.numpy as jnp
from jax import lax

HOURS = 24
K = 256
BLK = 128
RT = 128
NB_DEV = 128
TCAP = 256
NRT = 2048
TILES = 8192
NREC = 262144
NCELLS = 524288
N_CELLS = 32
N_RCPT = 4


def draw_tile_count(key, part):
    low_key = jax.random.fold_in(key, 11)
    top_key = jax.random.fold_in(key, 12)
    counts = jax.random.randint(low_key, (N_RCPT, N_CELLS), TCAP // 8, TCAP // 2 + 1)
    busiest = jax.random.randint(top_key, (N_RCPT, 1), 0, N_CELLS)
    device_ids = jnp.arange(N_CELLS, dtype=jnp.int32)[None, :]
    return jnp.where(device_ids == busiest, TCAP, counts).astype(jnp.int32)


def shuffle_labels(row_key):
    labels = jnp.arange(TCAP, dtype=jnp.int32) % N_CELLS
    return jax.random.permutation(row_key, labels)


def draw_tile_row(key, part):
    share_tiles = NRT // N_CELLS
    row_keys = jax.random.split(jax.random.fold_in(key, 21), N_RCPT * N_CELLS)
    owners = jax.vmap(shuffle_labels)(row_keys)
    within = jax.random.randint(jax.random.fold_in(key, 22), (N_RCPT * N_CELLS, TCAP), 0, share_tiles)
    return (owners * share_tiles + within).reshape(N_RCPT, TILES).astype(jnp.int32)


def set_ends(drawn, stream_key, least, largest):
    extent = drawn.shape
    index_at = [jax.random.randint(jax.random.fold_in(stream_key, axis), (), 0, extent[axis]) for axis in range(len(extent))]
    drawn = drawn.at[tuple(index_at)].set(least)
    longest = extent.index(max(extent))
    index_at[longest] = (index_at[longest] + 1) % extent[longest]
    return drawn.at[tuple(index_at)].set(largest)


def block_levels(rng, dims, cuts, least, top_value):
    gain = 1.0
    for dim, parts in cuts:
        draws = jax.random.uniform(jax.random.fold_in(jax.random.fold_in(rng, 6), dim), (parts,), jnp.float32, least / len(cuts), top_value / len(cuts))
        gain = gain * jnp.repeat(jnp.exp(draws), dims[dim] // parts).reshape((-1,) + (1,) * (len(dims) - 1 - dim))
    return gain


def gaussian(key, shape, scale, reach, shards=(), kind=jnp.bfloat16):
    gain = block_levels(key, shape, shards, -0.22, 0.18) if shards else 1.0
    array = jax.random.normal(key, shape, jnp.float32) * scale * gain
    return jnp.minimum(jnp.maximum(array, -reach), reach).astype(kind)


def setup_inputs(seed: int = 0) -> dict:
    streams_of = jax.random.split(jax.random.key(seed), 11)
    control = gaussian(streams_of[0], (HOURS, K), 0.5, 3.0, (), jnp.float32)
    background = jnp.clip(jnp.exp(math.log(3.0) - 2.3025851 * jax.random.uniform(streams_of[1], (HOURS, NCELLS), jnp.float32) ** block_levels(streams_of[1], (HOURS, NCELLS), ((1, 32),), -0.2, 0.2)), 0.3, 3.0)
    ensemble = gaussian(streams_of[2], (K, NCELLS), (0.8 * K ** -0.5), 0.3125, ((1, 32),))
    footprint = jnp.clip(jnp.exp(math.log(0.0234375) - 4.6082674 * jax.random.uniform(streams_of[3], (N_RCPT, TILES, RT, BLK), jnp.float32) ** block_levels(streams_of[3], (N_RCPT, TILES, RT, BLK), ((0, 4), (1, 32)), -0.2, 0.2)), 0.00023365021, 0.0234375).astype(jnp.bfloat16)
    tile_block = set_ends(jax.random.randint(streams_of[4], (N_RCPT, TILES), 0, NB_DEV), jax.random.fold_in(streams_of[4], 1), 0, NB_DEV - 1).astype(jnp.int32)
    tile_row = draw_tile_row(jax.random.fold_in(streams_of[10], 71), 0)
    tile_count = draw_tile_count(jax.random.fold_in(streams_of[10], 71), 0)
    hour = set_ends(jax.random.randint(streams_of[7], (N_RCPT, NREC), 0, HOURS), jax.random.fold_in(streams_of[7], 1), 0, HOURS - 1).astype(jnp.int32)
    observed = gaussian(streams_of[8], (N_RCPT, NREC), 1.0, 6.0, ((0, 4),), jnp.float32)
    inv_var = jnp.clip(jnp.exp(math.log(4.0) - 2.0794415 * jax.random.uniform(streams_of[9], (N_RCPT, NREC), jnp.float32) ** block_levels(streams_of[9], (N_RCPT, NREC), ((0, 4),), -0.2, 0.2)), 0.5, 4.0)
    return dict(control=control, background=background, ensemble=ensemble, footprint=footprint, tile_block=tile_block, tile_row=tile_row, tile_count=tile_count, hour=hour, observed=observed, inv_var=inv_var)


step_size = 0.5


def hour_onehot(hour_ids):
    return (hour_ids[..., None] == jnp.arange(HOURS, dtype=jnp.int32)).astype(jnp.float32)


def batched(values, batch_size):
    return values.reshape((TILES // batch_size, batch_size) + values.shape[1:])


def group_forward(emission, tiles, global_blocks, tile_rows, is_live, hour_tab):
    batch_size = math.gcd(TILES, 256)

    def one_batch(modelled, batch_item):
        tile_part, block_part, row_part, live_part = batch_item
        block_emis = jnp.take(emission, block_part, axis=1).astype(jnp.float32)
        product = jnp.einsum("gib,hgb->gih", tile_part.astype(jnp.float32), block_emis)
        contrib = jnp.sum(product * hour_onehot(hour_tab[row_part]), axis=2) * live_part[:, None]
        return modelled.at[row_part].add(contrib), None

    stacked = (batched(tiles, batch_size), batched(global_blocks, batch_size), batched(tile_rows, batch_size), batched(is_live, batch_size))
    modelled, unused = lax.scan(one_batch, jnp.zeros((NRT, RT), jnp.float32), stacked)
    return modelled.reshape(NREC)


def group_adjoint(tiles, global_blocks, tile_rows, is_live, hour_tab, departure_tab):
    batch_size = math.gcd(TILES, 256)

    def one_batch(adjoint, batch_item):
        tile_part, block_part, row_part, live_part = batch_item
        weighted = hour_onehot(hour_tab[row_part]) * departure_tab[row_part][:, :, None].astype(jnp.float32)
        adj_part = jnp.einsum("gih,gib->hgb", weighted, tile_part.astype(jnp.float32)) * live_part[None, :, None]
        return adjoint.at[:, block_part].add(adj_part), None

    stacked = (batched(tiles, batch_size), batched(global_blocks, batch_size), batched(tile_rows, batch_size), batched(is_live, batch_size))
    adjoint, unused = lax.scan(one_batch, jnp.zeros((HOURS, NCELLS // BLK, BLK), jnp.float32), stacked)
    return adjoint


def evaluate(control_now, background, ensemble, footprint, global_blocks, tile_row, is_live, hour, observed, inv_var):
    ensemble_part = jnp.dot(control_now.astype(jnp.bfloat16), ensemble, preferred_element_type=jnp.float32)
    emission = (background + ensemble_part).astype(jnp.bfloat16).reshape(HOURS, NCELLS // BLK, BLK)
    gradient = control_now
    concentrations = []
    for group_idx in range(N_RCPT):
        hour_tab = hour[group_idx].reshape(NRT, RT)
        modelled = group_forward(emission, footprint[group_idx], global_blocks[group_idx], tile_row[group_idx], is_live[group_idx], hour_tab)
        departure = (inv_var[group_idx] * (modelled - observed[group_idx])).astype(jnp.bfloat16)
        adjoint = group_adjoint(footprint[group_idx], global_blocks[group_idx], tile_row[group_idx], is_live[group_idx], hour_tab, departure.reshape(NRT, RT))
        rounded = adjoint.reshape(HOURS, NCELLS).astype(jnp.bfloat16)
        gradient = gradient + lax.dot_general(rounded, ensemble, (((1,), (1,)), ((), ())), preferred_element_type=jnp.float32)
        concentrations.append(modelled)
    return gradient, jnp.stack(concentrations)


def reference(control, background, ensemble, footprint, tile_block, tile_row, tile_count, hour, observed, inv_var):
    slot_ids = jnp.arange(TILES, dtype=jnp.int32)
    owner_ids = slot_ids // TCAP
    is_live = ((slot_ids % TCAP)[None, :] < tile_count[:, owner_ids]).astype(jnp.float32)
    global_blocks = (owner_ids * NB_DEV)[None, :] + tile_block
    first_grad, unused = evaluate(control, background, ensemble, footprint, global_blocks, tile_row, is_live, hour, observed, inv_var)
    updated = control - step_size * first_grad
    second_grad, concentrations = evaluate(updated, background, ensemble, footprint, global_blocks, tile_row, is_live, hour, observed, inv_var)
    return jnp.stack([first_grad, second_grad]), concentrations
```

```python
import jax
import jax.numpy as jnp
from jax import lax
from jax.experimental import pallas as pl
from jax.experimental.pallas import tpu as pltpu
from jax.sharding import Mesh
from jax.sharding import PartitionSpec as P

CELLS = ("cells_0", "cells_1", "cells_2")
PLANE = ("cells_0", "cells_1")
REST = ("cells_2", "rcpt")

step_size = 0.5

ENS_CHUNKS = 8
TILE_CHUNK = 32
UNROLL = 8
F32 = jnp.float32
BF16 = jnp.bfloat16


def from_everyone(value, axis):
    copies = jnp.broadcast_to(value, (lax.axis_size(axis), *value.shape))
    return lax.all_to_all(copies, axis, split_axis=0, concat_axis=0, tiled=True)


def copy_into(source, target, sem):
    return pltpu.make_async_copy(source, target, sem)


def forward_kernel(
    meta, weights, background, ensemble, footprint, hour,
    out, ens_buf, bg_buf, tile_buf, hour_buf, emis, partial, row_ids,
    ens_sem, bg_sem, tile_sem, hour_sem,
):
    slots = tile_buf.shape[0]
    hours = weights.shape[0]
    width = ens_buf.shape[2]
    blocks = width // 128
    live = meta[3 * slots]
    chunks = slots // TILE_CHUNK

    def ens_copy(c):
        return copy_into(ensemble.at[:, pl.ds(c * width, width)], ens_buf.at[c], ens_sem.at[c])

    def bg_copy(c):
        return copy_into(background.at[:, pl.ds(c * width, width)], bg_buf.at[c], bg_sem.at[c])

    def tile_copy(c):
        part = pl.ds(c * TILE_CHUNK, TILE_CHUNK)
        return copy_into(footprint.at[part], tile_buf.at[part], tile_sem.at[c])

    for c in range(ENS_CHUNKS):
        ens_copy(c).start()
        bg_copy(c).start()
    hour_copy = copy_into(hour, hour_buf, hour_sem)
    hour_copy.start()
    for c in range(chunks):
        @pl.when(c * TILE_CHUNK < live)
        def _():
            tile_copy(c).start()

    partial[...] = jnp.zeros_like(partial)
    row_ids[...] = jnp.zeros_like(row_ids)
    scaled = weights[...].astype(BF16)
    for c in range(ENS_CHUNKS):
        ens_copy(c).wait()
        bg_copy(c).wait()
        values = bg_buf[c] + jnp.dot(scaled, ens_buf[c], preferred_element_type=F32)
        values = values.astype(BF16)
        for b in range(blocks):
            emis[c * blocks + b] = values[:, b * 128 : (b + 1) * 128]
    hour_copy.wait()
    hour_line = lax.broadcasted_iota(jnp.int32, (hours, 128), 0)

    for c in range(chunks):
        @pl.when(c * TILE_CHUNK < live)
        def _():
            tile_copy(c).wait()

            def some_slots(g, carry):
                for u in range(UNROLL):
                    s = c * TILE_CHUNK + g * UNROLL + u
                    row = meta[slots + s]
                    place = meta[2 * slots + s]
                    every = lax.dot_general(
                        emis[meta[s]], tile_buf[s], (((1,), (1,)), ((), ())),
                        preferred_element_type=F32,
                    )
                    chosen = (hour_line == hour_buf[pl.ds(row, 1), :]) & (s < live)
                    line = jnp.sum(jnp.where(chosen, every, 0.0), axis=0, keepdims=True)
                    partial[pl.ds(place, 1), :] = line
                    row_ids[pl.ds(place, 1), :] = jnp.full((1, 128), (row % 64).astype(F32))
                return carry

            here = jnp.minimum(live - c * TILE_CHUNK, TILE_CHUNK)
            lax.fori_loop(0, (here + UNROLL - 1) // UNROLL, some_slots, 0)

    both = jnp.concatenate(
        [partial[...].reshape(slots // 8, 8, 128), row_ids[...].reshape(slots // 8, 8, 128)], axis=1
    )
    out[...] = both.astype(BF16)


def departure_kernel(position, received, observed, inv_var, modelled, send):
    tiles = modelled.shape[0]
    senders = received.shape[0]
    both = received[...].astype(F32)
    data = both[:, 0:8, :].reshape(senders * 8, 128).astype(BF16)
    ids = both[:, 8:16, 0:tiles].reshape(senders * 8, tiles)
    lane = lax.broadcasted_iota(jnp.int32, ids.shape, 1).astype(F32)
    pick = jnp.where(ids == lane, 1.0, 0.0).astype(BF16)
    own = lax.dot_general(pick, data, (((0,), (0,)), ((), ())), preferred_element_type=F32)
    modelled[...] = own
    departure = (inv_var[...] * (own - observed[...])).astype(BF16)
    send[...] = jnp.dot(pick, departure, preferred_element_type=F32).astype(BF16)


def adjoint_kernel(
    meta, departures, ensemble, footprint, hour,
    out, ens_buf, tile_buf, hour_buf, dep_buf, adjoint,
    ens_sem, tile_sem, hour_sem,
):
    slots = tile_buf.shape[0]
    hours = out.shape[0]
    width = ens_buf.shape[2]
    blocks = width // 128
    live = meta[3 * slots]
    chunks = slots // TILE_CHUNK

    def ens_copy(c):
        return copy_into(ensemble.at[:, pl.ds(c * width, width)], ens_buf.at[c], ens_sem.at[c])

    def tile_copy(c):
        part = pl.ds(c * TILE_CHUNK, TILE_CHUNK)
        return copy_into(footprint.at[part], tile_buf.at[part], tile_sem.at[c])

    hour_copy = copy_into(hour, hour_buf, hour_sem)
    hour_copy.start()
    for c in range(chunks):
        @pl.when(c * TILE_CHUNK < live)
        def _():
            tile_copy(c).start()
    for c in range(ENS_CHUNKS):
        ens_copy(c).start()

    dep_buf[...] = departures[...].astype(F32)
    adjoint[...] = jnp.zeros_like(adjoint)
    hour_copy.wait()
    hour_line = lax.broadcasted_iota(jnp.int32, (hours, 128), 0)

    for c in range(chunks):
        @pl.when(c * TILE_CHUNK < live)
        def _():
            tile_copy(c).wait()

            def some_slots(g, carry):
                for u in range(UNROLL):
                    s = c * TILE_CHUNK + g * UNROLL + u
                    block = meta[s]
                    chosen = (hour_line == hour_buf[pl.ds(meta[slots + s], 1), :]) & (s < live)
                    weighted = jnp.where(chosen, dep_buf[pl.ds(meta[2 * slots + s], 1), :], 0.0)
                    adjoint[block] += jnp.dot(
                        weighted.astype(BF16), tile_buf[s], preferred_element_type=F32
                    )
                return carry

            here = jnp.minimum(live - c * TILE_CHUNK, TILE_CHUNK)
            lax.fori_loop(0, (here + UNROLL - 1) // UNROLL, some_slots, 0)

    total = jnp.zeros(out.shape, F32)
    for c in range(ENS_CHUNKS):
        ens_copy(c).wait()
        rounded = jnp.concatenate([adjoint[c * blocks + b] for b in range(blocks)], axis=1)
        total = total + lax.dot_general(
            rounded.astype(BF16), ens_buf[c], (((1,), (1,)), ((), ())), preferred_element_type=F32
        )
    out[...] = total


def per_device(
    control, background, ensemble, footprint, tile_block, tile_row, tile_count, hour, observed, inv_var,
):
    hours, members = control.shape
    cells_dev = background.shape[1]
    slots = footprint.shape[1]
    receptors = hour.shape[1]
    row_tiles = receptors // 128
    devices = lax.axis_size(CELLS)
    share_tiles = row_tiles // devices
    width = cells_dev // ENS_CHUNKS
    chunks = slots // TILE_CHUNK

    hour_tab = hour.reshape(row_tiles, 128)
    obs_tab = observed.reshape(row_tiles, 128)
    var_tab = inv_var.reshape(row_tiles, 128)
    tiles = footprint[0]
    rows = tile_row[0]
    owner = rows // share_tiles
    order = jnp.arange(slots, dtype=jnp.int32)
    earlier = (owner[None, :] == owner[:, None]) & (order[None, :] < order[:, None])
    place = owner * (slots // devices) + jnp.sum(earlier.astype(jnp.int32), axis=1)
    meta = jnp.concatenate([tile_block[0], rows, place, tile_count[0]])
    position = lax.axis_index(CELLS).astype(jnp.int32).reshape(1)

    smem = pl.BlockSpec(memory_space=pltpu.SMEM)
    vmem = pl.BlockSpec(memory_space=pltpu.VMEM)
    hbm = pl.BlockSpec(memory_space=pl.ANY)

    forward = pl.pallas_call(
        forward_kernel,
        out_shape=jax.ShapeDtypeStruct((devices, 16, 128), BF16),
        in_specs=[smem, vmem, hbm, hbm, hbm, hbm],
        out_specs=vmem,
        scratch_shapes=[
            pltpu.VMEM((ENS_CHUNKS, members, width), BF16),
            pltpu.VMEM((ENS_CHUNKS, hours, width), F32),
            pltpu.VMEM((slots, 128, 128), BF16),
            pltpu.VMEM((row_tiles, 128), jnp.int32),
            pltpu.VMEM((cells_dev // 128, hours, 128), BF16),
            pltpu.VMEM((slots, 128), F32),
            pltpu.VMEM((slots, 128), F32),
            pltpu.SemaphoreType.DMA((ENS_CHUNKS,)),
            pltpu.SemaphoreType.DMA((ENS_CHUNKS,)),
            pltpu.SemaphoreType.DMA((chunks,)),
            pltpu.SemaphoreType.DMA,
        ],
        name="forward",
    )

    share = pl.BlockSpec((share_tiles, 128), lambda i, p: (p[0], 0))
    depart = pl.pallas_call(
        departure_kernel,
        out_shape=(
            jax.ShapeDtypeStruct((share_tiles, 128), F32),
            jax.ShapeDtypeStruct((slots, 128), BF16),
        ),
        grid_spec=pltpu.PrefetchScalarGridSpec(
            num_scalar_prefetch=1,
            grid=(1,),
            in_specs=[pl.BlockSpec((devices, 16, 128), lambda i, p: (0, 0, 0)), share, share],
            out_specs=[
                pl.BlockSpec((share_tiles, 128), lambda i, p: (0, 0)),
                pl.BlockSpec((slots, 128), lambda i, p: (0, 0)),
            ],
        ),
        name="depart",
    )

    adjoint = pl.pallas_call(
        adjoint_kernel,
        out_shape=jax.ShapeDtypeStruct((hours, members), F32),
        in_specs=[smem, vmem, hbm, hbm, hbm],
        out_specs=vmem,
        scratch_shapes=[
            pltpu.VMEM((ENS_CHUNKS, members, width), BF16),
            pltpu.VMEM((slots, 128, 128), BF16),
            pltpu.VMEM((row_tiles, 128), jnp.int32),
            pltpu.VMEM((slots, 128), F32),
            pltpu.VMEM((cells_dev // 128, hours, 128), F32),
            pltpu.SemaphoreType.DMA((ENS_CHUNKS,)),
            pltpu.SemaphoreType.DMA((chunks,)),
            pltpu.SemaphoreType.DMA,
        ],
        name="adjoint",
    )

    def evaluate(control_now):
        partials = forward(meta, control_now, background, ensemble, tiles, hour_tab)
        received = lax.all_to_all(partials, CELLS, 0, 0, tiled=True)
        modelled, send = depart(position, received, obs_tab, var_tab)
        send = send.reshape(devices, slots // devices, 128)
        back = lax.all_to_all(send, CELLS, 0, 0, tiled=True).reshape(slots, 128)
        local = adjoint(meta, back, ensemble, tiles, hour_tab)
        plane = from_everyone(local.astype(BF16), PLANE)
        partly = jnp.sum(plane.astype(F32), axis=0).astype(BF16)
        rest = from_everyone(partly, REST)
        gradient = control_now + jnp.sum(rest.astype(F32), axis=0)
        return gradient, modelled

    first_grad, unused = evaluate(control)
    second_grad, final = evaluate(control - step_size * first_grad)
    return jnp.stack([first_grad, second_grad]), final.reshape(1, receptors // devices)


def solution(mesh):
    torus = Mesh(
        mesh.devices.reshape(4, 4, 2, mesh.shape["rcpt"]), ("cells_0", "cells_1", "cells_2", "rcpt")
    )
    return jax.shard_map(
        per_device,
        mesh=torus,
        in_specs=(
            P(),
            P(None, CELLS),
            P(None, CELLS),
            P("rcpt", CELLS, None, None),
            P("rcpt", CELLS),
            P("rcpt", CELLS),
            P("rcpt", CELLS),
            P("rcpt", None),
            P("rcpt", None),
            P("rcpt", None),
        ),
        out_specs=(P(), P("rcpt", CELLS)),
        check_vma=False,
    )
```

```python
import jax
import jax.numpy as jnp
from jax import lax
from jax.experimental import pallas as pl
from jax.experimental.pallas import tpu as pltpu
from jax.sharding import Mesh
from jax.sharding import PartitionSpec as P

CELLS = ("cells_0", "cells_1", "cells_2")
PLANE = ("cells_0", "cells_1")
REST = ("cells_2", "rcpt")

step_size = 0.5

ENS_CHUNKS = 8
TILE_CHUNK = 32
UNROLL = 8
F32 = jnp.float32
BF16 = jnp.bfloat16
I32 = jnp.int32


def slot_places(rows, share_tiles, per_share):
    slots = rows.shape[1]
    owner = jnp.broadcast_to(rows // share_tiles, (slots, slots))
    down = lax.broadcasted_iota(I32, (slots, slots), 0)
    across = lax.broadcasted_iota(I32, (slots, slots), 1)
    column = jnp.sum(jnp.where(down == across, owner, 0), axis=1, keepdims=True)
    earlier = (owner == column) & (down < across)
    rank = jnp.sum(earlier.astype(I32), axis=0, keepdims=True)
    return (rows // share_tiles) * per_share + rank


def emissions(scaled, background, ensemble, emis, c):
    blocks = ensemble.shape[2] // 128
    values = background[c] + jnp.dot(scaled, ensemble[c], preferred_element_type=F32)
    values = values.astype(BF16).astype(F32)
    for b in range(blocks):
        emis[c * blocks + b] = values[:, b * 128 : (b + 1) * 128]


def live_groups(live, work):
    lax.fori_loop(0, (live + UNROLL - 1) // UNROLL, lambda g, carry: (work(g), carry)[1], 0)


def forward_group(g, live, block, place, tiles, hour_rows, emis, partial):
    hours = emis.shape[1]
    hour_line = lax.broadcasted_iota(I32, (hours, 128), 0)
    none = jnp.zeros((hours, 128), F32)
    base = pl.multiple_of(g * UNROLL, UNROLL)
    these = hour_rows[pl.ds(base, UNROLL), :]
    for u in range(0, UNROLL, 2):
        s = base + u
        left = jnp.concatenate([emis[block[0, s]], none], axis=1)
        right = jnp.concatenate([none, emis[block[0, s + 1]]], axis=1)
        pair = jnp.concatenate([left, right], axis=0).astype(BF16)
        both = jnp.concatenate([tiles[s], tiles[s + 1]], axis=1)
        every = lax.dot_general(pair, both, (((1,), (1,)), ((), ())), preferred_element_type=F32)
        for v in range(2):
            chosen = (hour_line == these[u + v : u + v + 1, :]) & (s + v < live)
            part = jnp.where(chosen, every[v * hours : (v + 1) * hours], 0.0)
            partial[pl.ds(place[0, s + v], 1), :] = jnp.sum(part, axis=0, keepdims=True)


def first_forward_kernel(
    position, block, row, count, row_line, control, background, ensemble, footprint, hour,
    out, place_out, hour_rows, bg_buf, ens_buf, tile_buf,
    place, hour_buf, emis, partial, row_ids, ens_sem, bg_sem, tile_sem, hour_sem, place_sem,
):
    slots = tile_buf.shape[0]
    width = ens_buf.shape[2]
    senders = out.shape[0]
    share_tiles = hour_buf.shape[0] // senders
    live = count[0, 0]
    chunks = slots // TILE_CHUNK

    def ens_copy(c):
        return pltpu.make_async_copy(
            ensemble.at[:, pl.ds(c * width, width)], ens_buf.at[c], ens_sem.at[c]
        )

    def bg_copy(c):
        return pltpu.make_async_copy(
            background.at[:, pl.ds(c * width, width)], bg_buf.at[c], bg_sem.at[c]
        )

    def tile_copy(c):
        part = pl.ds(c * TILE_CHUNK, TILE_CHUNK)
        return pltpu.make_async_copy(footprint.at[part], tile_buf.at[part], tile_sem.at[c])

    for c in range(ENS_CHUNKS):
        ens_copy(c).start()
        bg_copy(c).start()
    hour_copy = pltpu.make_async_copy(hour, hour_buf, hour_sem)
    hour_copy.start()
    for c in range(chunks):
        @pl.when(c * TILE_CHUNK < live)
        def _():
            tile_copy(c).start()

    place_out[...] = slot_places(row_line[...], share_tiles, slots // senders)
    place_copy = pltpu.make_async_copy(place_out, place, place_sem)
    place_copy.start()
    partial[...] = jnp.zeros_like(partial)
    row_ids[...] = jnp.zeros_like(row_ids)

    scaled = control[...].astype(BF16)
    for c in range(ENS_CHUNKS):
        ens_copy(c).wait()
        bg_copy(c).wait()
        emissions(scaled, bg_buf, ens_buf, emis, c)
    place_copy.wait()
    hour_copy.wait()
    for c in range(chunks):
        @pl.when(c * TILE_CHUNK < live)
        def _():
            tile_copy(c).wait()

    def work(g):
        for u in range(UNROLL):
            s = g * UNROLL + u
            here = row[0, s]
            hour_rows[pl.ds(s, 1), :] = hour_buf[pl.ds(here, 1), :]
            number = (here & (share_tiles - 1)).astype(F32)
            row_ids[pl.ds(place[0, s], 1), :] = jnp.full((1, 128), number)
        forward_group(g, live, block, place, tile_buf, hour_rows, emis, partial)

    live_groups(live, work)
    data = partial[...].reshape(senders, slots // senders, 128)
    ids = row_ids[...].reshape(senders, slots // senders, 128)
    out[...] = jnp.concatenate([data, ids], axis=1).astype(BF16)


def next_forward_kernel(
    block, place, count, control, copies, hour_rows, bg_buf, ens_buf, tile_buf,
    out, gradient, emis, partial,
):
    live = count[0, 0]
    slots = tile_buf.shape[0]
    senders = out.shape[0]
    total = control[...] + jnp.sum(copies[...].astype(F32), axis=0)
    gradient[...] = total
    scaled = (control[...] - step_size * total).astype(BF16)
    partial[...] = jnp.zeros_like(partial)
    for c in range(ENS_CHUNKS):
        emissions(scaled, bg_buf, ens_buf, emis, c)
    live_groups(
        live, lambda g: forward_group(g, live, block, place, tile_buf, hour_rows, emis, partial)
    )
    data = partial[...].reshape(senders, slots // senders, 128)
    rounded = data.astype(BF16).astype(F32)
    out[...] = jnp.concatenate([rounded, data - rounded], axis=1).astype(BF16)


def owner_pick(received, tiles):
    ids = received[...].astype(F32)[:, 8:16, 0:tiles].reshape(received.shape[0] * 8, tiles)
    lane = lax.broadcasted_iota(I32, ids.shape, 1).astype(F32)
    return jnp.where(ids == lane, 1.0, 0.0).astype(BF16)


def picked_sum(pick, part):
    part = part.reshape(pick.shape[0], 128).astype(BF16)
    return lax.dot_general(pick, part, (((0,), (0,)), ((), ())), preferred_element_type=F32)


def first_departure_kernel(position, received, observed, inv_var, send):
    pick = owner_pick(received, observed.shape[0])
    own = picked_sum(pick, received[...].astype(F32)[:, 0:8, :])
    departure = (inv_var[...] * (own - observed[...])).astype(BF16)
    send[...] = jnp.dot(pick, departure, preferred_element_type=F32).astype(BF16)


def next_departure_kernel(position, named, received, observed, inv_var, modelled, send):
    pick = owner_pick(named, observed.shape[0])
    both = received[...].astype(F32)
    own = picked_sum(pick, both[:, 0:8, :]) + picked_sum(pick, both[:, 8:16, :])
    modelled[...] = own
    departure = (inv_var[...] * (own - observed[...])).astype(BF16)
    send[...] = jnp.dot(pick, departure, preferred_element_type=F32).astype(BF16)


def adjoint_kernel(
    block, place, count, departures, hour_rows, ens_buf, tile_buf, out, dep_buf, adjoint
):
    hours = out.shape[1]
    blocks = ens_buf.shape[2] // 128
    live = count[0, 0]
    hour_line = lax.broadcasted_iota(I32, (hours, 128), 0)
    dep_buf[...] = departures[...].astype(F32)
    adjoint[...] = jnp.zeros_like(adjoint)

    def work(g):
        base = pl.multiple_of(g * UNROLL, UNROLL)
        these = hour_rows[pl.ds(base, UNROLL), :]
        for u in range(0, UNROLL, 2):
            s = base + u
            weighted = []
            for v in range(2):
                chosen = (hour_line == these[u + v : u + v + 1, :]) & (s + v < live)
                weighted.append(jnp.where(chosen, dep_buf[pl.ds(place[0, s + v], 1), :], 0.0))
            pair = jnp.concatenate(weighted, axis=0).astype(BF16)
            both = jnp.concatenate([tile_buf[s], tile_buf[s + 1]], axis=1)
            every = jnp.dot(pair, both, preferred_element_type=F32)
            adjoint[block[0, s]] += every[0:hours, 0:128]
            adjoint[block[0, s + 1]] += every[hours : 2 * hours, 128:256]

    live_groups(live, work)
    total = jnp.zeros(out.shape[1:], F32)
    for c in range(ENS_CHUNKS):
        rounded = jnp.concatenate([adjoint[c * blocks + b] for b in range(blocks)], axis=1)
        total = total + lax.dot_general(
            rounded.astype(BF16), ens_buf[c], (((1,), (1,)), ((), ())), preferred_element_type=F32
        )
    total = total.astype(BF16)
    for j in range(out.shape[0]):
        out[j] = total


def exchange(value, axes):
    return lax.all_to_all(value, axes, 0, 0, tiled=True)


def per_device(
    control, background, ensemble, footprint, tile_block, tile_row, tile_count, hour, observed, inv_var,
):
    hours, members = control.shape
    cells_dev = background.shape[1]
    slots = footprint.shape[1]
    receptors = hour.shape[1]
    row_tiles = receptors // 128
    devices = lax.axis_size(CELLS)
    plane = lax.axis_size(PLANE)
    rest = lax.axis_size(REST)
    share_tiles = row_tiles // devices
    width = cells_dev // ENS_CHUNKS
    chunks = slots // TILE_CHUNK

    hour_tab = hour.reshape(row_tiles, 128)
    obs_tab = observed.reshape(row_tiles, 128)
    var_tab = inv_var.reshape(row_tiles, 128)
    position = lax.axis_index(CELLS).astype(I32).reshape(1)

    smem = pl.BlockSpec(memory_space=pltpu.SMEM)
    vmem = pl.BlockSpec(memory_space=pltpu.VMEM)
    hbm = pl.BlockSpec(memory_space=pl.ANY)
    limit = pltpu.CompilerParams(vmem_limit_bytes=24 * 1024 * 1024)
    emis = pltpu.VMEM((cells_dev // 128, hours, 128), F32)
    slot_lines = pltpu.VMEM((slots, 128), F32)

    first_forward = pl.pallas_call(
        first_forward_kernel,
        out_shape=(
            pltpu.VMEM((devices, 16, 128), BF16),
            pltpu.VMEM((1, slots), I32),
            pltpu.VMEM((slots, 128), I32),
            pltpu.VMEM((ENS_CHUNKS, hours, width), F32),
            pltpu.VMEM((ENS_CHUNKS, members, width), BF16),
            pltpu.VMEM((slots, 128, 128), BF16),
        ),
        in_specs=[smem, smem, smem, smem, vmem, vmem, hbm, hbm, hbm, hbm],
        out_specs=(vmem,) * 6,
        scratch_shapes=[
            pltpu.SMEM((1, slots), I32),
            pltpu.VMEM((row_tiles, 128), I32),
            emis,
            slot_lines,
            slot_lines,
            pltpu.SemaphoreType.DMA((ENS_CHUNKS,)),
            pltpu.SemaphoreType.DMA((ENS_CHUNKS,)),
            pltpu.SemaphoreType.DMA((chunks,)),
            pltpu.SemaphoreType.DMA,
            pltpu.SemaphoreType.DMA,
        ],
        compiler_params=limit,
        name="first_forward",
    )
    next_forward = pl.pallas_call(
        next_forward_kernel,
        out_shape=(
            pltpu.VMEM((devices, 16, 128), BF16),
            jax.ShapeDtypeStruct((hours, members), F32),
        ),
        in_specs=[smem, smem, smem] + [vmem] * 6,
        out_specs=(vmem, vmem),
        scratch_shapes=[emis, slot_lines],
        compiler_params=limit,
        name="next_forward",
    )

    share = pl.BlockSpec((share_tiles, 128), lambda i, p: (p[0], 0))
    sent = pltpu.VMEM((slots, 128), BF16)
    own = jax.ShapeDtypeStruct((share_tiles, 128), F32)

    def depart(kernel, arrays, out_shape, name):
        return pl.pallas_call(
            kernel,
            out_shape=out_shape,
            grid_spec=pltpu.PrefetchScalarGridSpec(
                num_scalar_prefetch=1,
                grid=(1,),
                in_specs=[vmem] * arrays + [share, share],
                out_specs=[vmem] * len(out_shape),
            ),
            compiler_params=pltpu.CompilerParams(vmem_limit_bytes=4 * 1024 * 1024),
            name=name,
        )

    adjoint = pl.pallas_call(
        adjoint_kernel,
        out_shape=pltpu.VMEM((rest, hours, members), BF16),
        in_specs=[smem, smem, smem] + [vmem] * 4,
        out_specs=vmem,
        scratch_shapes=[slot_lines, emis],
        compiler_params=limit,
        name="adjoint",
    )

    def summed(send, place, hour_rows, ens_buf, tile_buf):
        back = exchange(send.reshape(devices, slots // devices, 128), CELLS).reshape(slots, 128)
        copies = adjoint(tile_block, place, tile_count, back, hour_rows, ens_buf, tile_buf)
        partly = jnp.sum(exchange(copies, REST).astype(F32), axis=0)
        partly = lax.optimization_barrier(partly).astype(BF16)
        return exchange(jnp.broadcast_to(partly, (plane, hours, members)), PLANE)

    large = [
        pltpu.with_memory_space_constraint(array, pltpu.HBM)
        for array in (background, ensemble, footprint[0], hour_tab)
    ]
    partials, place, hour_rows, bg_buf, ens_buf, tile_buf = first_forward(
        position, tile_block, tile_row, tile_count, tile_row, control, *large
    )
    named = exchange(partials, CELLS)
    (send,) = depart(first_departure_kernel, 1, (sent,), "first_departure")(
        position, named, obs_tab, var_tab
    )
    copies = summed(send, place, hour_rows, ens_buf, tile_buf)
    partials, first_grad = next_forward(
        tile_block, place, tile_count, control, copies, hour_rows, bg_buf, ens_buf, tile_buf
    )
    received = exchange(partials, CELLS)
    final, send = depart(next_departure_kernel, 2, (own, sent), "next_departure")(
        position, named, received, obs_tab, var_tab
    )
    copies = summed(send, place, hour_rows, ens_buf, tile_buf)
    updated = control - step_size * first_grad
    second_grad = updated + jnp.sum(copies.astype(F32), axis=0)
    return jnp.stack([first_grad, second_grad]), final.reshape(1, receptors // devices)


def solution(mesh):
    torus = Mesh(
        mesh.devices.reshape(4, 4, 2, mesh.shape["rcpt"]), ("cells_0", "cells_1", "cells_2", "rcpt")
    )
    return jax.shard_map(
        per_device,
        mesh=torus,
        in_specs=(
            P(),
            P(None, CELLS),
            P(None, CELLS),
            P("rcpt", CELLS, None, None),
            P("rcpt", CELLS),
            P("rcpt", CELLS),
            P("rcpt", CELLS),
            P("rcpt", None),
            P("rcpt", None),
            P("rcpt", None),
        ),
        out_specs=(P(), P("rcpt", CELLS)),
        check_vma=False,
    )
```

```python
import jax
import jax.numpy as jnp
from jax import lax
from jax.experimental import pallas as pl
from jax.experimental.pallas import tpu as pltpu
from jax.sharding import Mesh
from jax.sharding import PartitionSpec as P

CELLS = ("cells_0", "cells_1", "cells_2")
PLANE = ("cells_0", "cells_1")
REST = ("cells_2", "rcpt")

step_size = 0.5

ENS_CHUNKS = 8
UNROLL = 32
F32 = jnp.float32
BF16 = jnp.bfloat16
I32 = jnp.int32


def slot_places(rows, share_tiles, per_share):
    slots = rows.shape[1]
    owner = jnp.broadcast_to(rows // share_tiles, (slots, slots))
    down = lax.broadcasted_iota(I32, (slots, slots), 0)
    across = lax.broadcasted_iota(I32, (slots, slots), 1)
    column = jnp.sum(jnp.where(down == across, owner, 0), axis=1, keepdims=True)
    earlier = (owner == column) & (down < across)
    rank = jnp.sum(earlier.astype(I32), axis=0, keepdims=True)
    return (rows // share_tiles) * per_share + rank


def emissions(scaled, background, ensemble, emis, c):
    blocks = ensemble.shape[2] // 128
    values = background[c] + jnp.dot(scaled, ensemble[c], preferred_element_type=F32)
    values = values.astype(BF16).astype(F32)
    for b in range(blocks):
        emis[c * blocks + b] = values[:, b * 128 : (b + 1) * 128]


def live_groups(live, work):
    lax.fori_loop(0, (live + UNROLL - 1) // UNROLL, lambda g, carry: (work(g), carry)[1], 0)


def split_halves(value):
    rounded = value.astype(BF16).astype(F32)
    return [rounded, value - rounded]


def forward_group(g, block, place, tiles, hour_rows, emis, partial):
    hours = emis.shape[1]
    hour_line = lax.broadcasted_iota(I32, (hours, 128), 0)
    none = jnp.zeros((hours, 128), F32)
    base = pl.multiple_of(g * UNROLL, UNROLL)
    these = hour_rows[pl.ds(base, UNROLL), :]
    for u in range(0, UNROLL, 2):
        s = base + u
        left = jnp.concatenate([emis[block[0, s]], none], axis=1)
        right = jnp.concatenate([none, emis[block[0, s + 1]]], axis=1)
        pair = jnp.concatenate([left, right], axis=0).astype(BF16)
        both = jnp.concatenate([tiles[s], tiles[s + 1]], axis=1)
        every = lax.dot_general(pair, both, (((1,), (1,)), ((), ())), preferred_element_type=F32)
        for v in range(2):
            chosen = hour_line == these[u + v : u + v + 1, :]
            part = jnp.where(chosen, every[v * hours : (v + 1) * hours], 0.0)
            partial[pl.ds(place[0, s + v], 1), :] = jnp.sum(part, axis=0, keepdims=True)


def first_forward_kernel(
    position, block, row, count, row_line, control, background, ensemble, footprint, hour,
    observed, inv_var,
    out, place_out, hour_rows, bg_buf, ens_buf, tile_buf, own_observed, own_inv_var,
    place, line_buf, control_buf, hour_buf, emis, partial, row_ids,
    ens_sem, bg_sem, tile_sem, hour_sem, place_sem, small_sem,
):
    slots = tile_buf.shape[0]
    width = ens_buf.shape[2]
    senders = out.shape[0]
    share_tiles = own_observed.shape[0]
    live = count[0, 0]
    chunks = slots // UNROLL

    def ens_copy(c):
        return pltpu.make_async_copy(
            ensemble.at[:, pl.ds(c * width, width)], ens_buf.at[c], ens_sem.at[c]
        )

    def bg_copy(c):
        return pltpu.make_async_copy(
            background.at[:, pl.ds(c * width, width)], bg_buf.at[c], bg_sem.at[c]
        )

    def tile_copy(c):
        part = pl.ds(c * UNROLL, UNROLL)
        return pltpu.make_async_copy(footprint.at[part], tile_buf.at[part], tile_sem.at[c])

    share = pl.ds(position[0] * share_tiles, share_tiles)
    small = [
        pltpu.make_async_copy(row_line, line_buf, small_sem.at[0]),
        pltpu.make_async_copy(control, control_buf, small_sem.at[1]),
        pltpu.make_async_copy(observed.at[share], own_observed, small_sem.at[2]),
        pltpu.make_async_copy(inv_var.at[share], own_inv_var, small_sem.at[3]),
    ]
    small[0].start()
    small[1].start()
    for c in range(ENS_CHUNKS):
        ens_copy(c).start()
        bg_copy(c).start()
    hour_copy = pltpu.make_async_copy(hour, hour_buf, hour_sem)
    hour_copy.start()
    for c in range(chunks):
        @pl.when(c * UNROLL < live)
        def _():
            tile_copy(c).start()
    small[2].start()
    small[3].start()

    small[0].wait()
    place_out[...] = slot_places(line_buf[...], share_tiles, slots // senders)
    place_copy = pltpu.make_async_copy(place_out, place, place_sem)
    place_copy.start()
    partial[...] = jnp.zeros_like(partial)
    row_ids[...] = jnp.zeros_like(row_ids)

    small[1].wait()
    scaled = control_buf[...].astype(BF16)
    for c in range(ENS_CHUNKS):
        ens_copy(c).wait()
        bg_copy(c).wait()
        emissions(scaled, bg_buf, ens_buf, emis, c)
    place_copy.wait()
    hour_copy.wait()

    def name_group(g):
        for u in range(UNROLL):
            s = g * UNROLL + u
            here = row[0, s]
            shown = hour_buf[pl.ds(here, 1), :]
            hour_rows[pl.ds(s, 1), :] = jnp.where(s < live, shown, -1)
            number = (here & (share_tiles - 1)).astype(F32)
            row_ids[pl.ds(place[0, s], 1), :] = jnp.full((1, 128), number)

    def work(g):
        name_group(g)
        tile_copy(g).wait()
        forward_group(g, block, place, tile_buf, hour_rows, emis, partial)

    live_groups(live, work)
    small[2].wait()
    small[3].wait()
    parts = split_halves(partial[...]) + [row_ids[...]]
    parts = [part.reshape(senders, slots // senders, 128) for part in parts]
    out[...] = jnp.concatenate(parts, axis=1).astype(BF16)


def next_forward_kernel(
    block, place, count, control, copies, hour_rows, bg_buf, ens_buf, tile_buf,
    out, gradient, emis, partial,
):
    live = count[0, 0]
    slots = tile_buf.shape[0]
    senders = out.shape[0]
    total = control[...] + jnp.sum(copies[...].astype(F32), axis=0)
    gradient[...] = total
    scaled = (control[...] - step_size * total).astype(BF16)
    partial[...] = jnp.zeros_like(partial)
    for c in range(ENS_CHUNKS):
        emissions(scaled, bg_buf, ens_buf, emis, c)
    live_groups(live, lambda g: forward_group(g, block, place, tile_buf, hour_rows, emis, partial))
    parts = [part.reshape(senders, slots // senders, 128) for part in split_halves(partial[...])]
    out[...] = jnp.concatenate(parts, axis=1).astype(BF16)


def owner_pick(received, tiles):
    ids = received[...].astype(F32)[:, 16:24, 0:tiles].reshape(received.shape[0] * 8, tiles)
    lane = lax.broadcasted_iota(I32, ids.shape, 1).astype(F32)
    return jnp.where(ids == lane, 1.0, 0.0).astype(BF16)


def own_sum(pick, received):
    both = received[...].astype(F32)
    own = None
    for first in (0, 8):
        part = both[:, first : first + 8, :].reshape(pick.shape[0], 128).astype(BF16)
        part = lax.dot_general(pick, part, (((0,), (0,)), ((), ())), preferred_element_type=F32)
        own = part if own is None else own + part
    return own


def send_departure(pick, own, observed, inv_var, send):
    departure = (inv_var[...] * (own - observed[...])).astype(BF16)
    send[...] = jnp.dot(pick, departure, preferred_element_type=F32).astype(BF16)


def first_departure_kernel(received, observed, inv_var, send):
    pick = owner_pick(received, observed.shape[0])
    send_departure(pick, own_sum(pick, received), observed, inv_var, send)


def next_departure_kernel(named, received, observed, inv_var, modelled, send):
    pick = owner_pick(named, observed.shape[0])
    own = own_sum(pick, received)
    modelled[...] = own
    send_departure(pick, own, observed, inv_var, send)


def adjoint_kernel(
    block, place, count, departures, hour_rows, ens_buf, tile_buf, out, dep_buf, adjoint
):
    hours = out.shape[1]
    blocks = ens_buf.shape[2] // 128
    live = count[0, 0]
    hour_line = lax.broadcasted_iota(I32, (hours, 128), 0)
    dep_buf[...] = departures[...].astype(F32)
    adjoint[...] = jnp.zeros_like(adjoint)

    def work(g):
        base = pl.multiple_of(g * UNROLL, UNROLL)
        these = hour_rows[pl.ds(base, UNROLL), :]
        for u in range(0, UNROLL, 2):
            s = base + u
            weighted = []
            for v in range(2):
                chosen = hour_line == these[u + v : u + v + 1, :]
                weighted.append(jnp.where(chosen, dep_buf[pl.ds(place[0, s + v], 1), :], 0.0))
            pair = jnp.concatenate(weighted, axis=0).astype(BF16)
            both = jnp.concatenate([tile_buf[s], tile_buf[s + 1]], axis=1)
            every = jnp.dot(pair, both, preferred_element_type=F32)
            adjoint[block[0, s]] += every[0:hours, 0:128]
            adjoint[block[0, s + 1]] += every[hours : 2 * hours, 128:256]

    live_groups(live, work)
    total = jnp.zeros(out.shape[1:], F32)
    for c in range(ENS_CHUNKS):
        rounded = jnp.concatenate([adjoint[c * blocks + b] for b in range(blocks)], axis=1)
        total = total + lax.dot_general(
            rounded.astype(BF16), ens_buf[c], (((1,), (1,)), ((), ())), preferred_element_type=F32
        )
    for j in range(out.shape[0]):
        out[j] = total


def sum_kernel(copies, out):
    total = jnp.sum(copies[...], axis=0).astype(BF16)
    for j in range(out.shape[0]):
        out[j] = total


def exchange(value, axes):
    return lax.all_to_all(value, axes, 0, 0, tiled=True)


def per_device(
    control, background, ensemble, footprint, tile_block, tile_row, tile_count, hour, observed, inv_var,
):
    hours, members = control.shape
    cells_dev = background.shape[1]
    slots = footprint.shape[1]
    receptors = hour.shape[1]
    row_tiles = receptors // 128
    devices = lax.axis_size(CELLS)
    plane = lax.axis_size(PLANE)
    rest = lax.axis_size(REST)
    share_tiles = row_tiles // devices
    width = cells_dev // ENS_CHUNKS

    hour_tab = hour.reshape(row_tiles, 128)
    obs_tab = observed.reshape(row_tiles, 128)
    var_tab = inv_var.reshape(row_tiles, 128)
    position = lax.axis_index(CELLS).astype(I32).reshape(1)

    smem = pl.BlockSpec(memory_space=pltpu.SMEM)
    vmem = pl.BlockSpec(memory_space=pltpu.VMEM)
    hbm = pl.BlockSpec(memory_space=pl.ANY)
    limit = pltpu.CompilerParams(vmem_limit_bytes=24 * 1024 * 1024)
    emis = pltpu.VMEM((cells_dev // 128, hours, 128), F32)
    slot_lines = pltpu.VMEM((slots, 128), F32)

    first_forward = pl.pallas_call(
        first_forward_kernel,
        out_shape=(
            pltpu.VMEM((devices, 24, 128), BF16),
            pltpu.VMEM((1, slots), I32),
            pltpu.VMEM((slots, 128), I32),
            pltpu.VMEM((ENS_CHUNKS, hours, width), F32),
            pltpu.VMEM((ENS_CHUNKS, members, width), BF16),
            pltpu.VMEM((slots, 128, 128), BF16),
            pltpu.VMEM((share_tiles, 128), F32),
            pltpu.VMEM((share_tiles, 128), F32),
        ),
        in_specs=[smem] * 4 + [hbm] * 8,
        out_specs=(vmem,) * 8,
        scratch_shapes=[
            pltpu.SMEM((1, slots), I32),
            pltpu.VMEM((1, slots), I32),
            pltpu.VMEM((hours, members), F32),
            pltpu.VMEM((row_tiles, 128), I32),
            emis,
            slot_lines,
            slot_lines,
            pltpu.SemaphoreType.DMA((ENS_CHUNKS,)),
            pltpu.SemaphoreType.DMA((ENS_CHUNKS,)),
            pltpu.SemaphoreType.DMA((slots // UNROLL,)),
            pltpu.SemaphoreType.DMA,
            pltpu.SemaphoreType.DMA,
            pltpu.SemaphoreType.DMA((4,)),
        ],
        compiler_params=limit,
        name="first_forward",
    )
    next_forward = pl.pallas_call(
        next_forward_kernel,
        out_shape=(
            pltpu.VMEM((devices, 16, 128), BF16),
            jax.ShapeDtypeStruct((hours, members), F32),
        ),
        in_specs=[smem, smem, smem] + [vmem] * 6,
        out_specs=(vmem, vmem),
        scratch_shapes=[emis, slot_lines],
        compiler_params=limit,
        name="next_forward",
    )

    sent = pltpu.VMEM((slots, 128), BF16)
    own = pltpu.VMEM((share_tiles, 128), F32)

    def depart(kernel, arrays, out_shape, name):
        return pl.pallas_call(
            kernel,
            out_shape=out_shape,
            in_specs=[vmem] * arrays,
            out_specs=(vmem,) * len(out_shape),
            compiler_params=pltpu.CompilerParams(vmem_limit_bytes=4 * 1024 * 1024),
            name=name,
        )

    adjoint = pl.pallas_call(
        adjoint_kernel,
        out_shape=pltpu.VMEM((rest, hours, members), F32),
        in_specs=[smem, smem, smem] + [vmem] * 4,
        out_specs=vmem,
        scratch_shapes=[slot_lines, emis],
        compiler_params=limit,
        name="adjoint",
    )

    add_copies = pl.pallas_call(
        sum_kernel,
        out_shape=pltpu.VMEM((plane, hours, members), BF16),
        in_specs=[vmem],
        out_specs=vmem,
        compiler_params=pltpu.CompilerParams(vmem_limit_bytes=4 * 1024 * 1024),
        name="add_copies",
    )

    def summed(send, place, hour_rows, ens_buf, tile_buf):
        back = exchange(send.reshape(devices, slots // devices, 128), CELLS).reshape(slots, 128)
        copies = adjoint(tile_block, place, tile_count, back, hour_rows, ens_buf, tile_buf)
        return exchange(add_copies(exchange(copies, REST)), PLANE)

    pinned = [
        pltpu.with_memory_space_constraint(array, pltpu.HBM)
        for array in (
            tile_row, control, background, ensemble, footprint[0], hour_tab, obs_tab, var_tab
        )
    ]
    partials, place, hour_rows, bg_buf, ens_buf, tile_buf, own_obs, own_var = first_forward(
        position, tile_block, tile_row, tile_count, *pinned
    )
    named = exchange(partials, CELLS)
    (send,) = depart(first_departure_kernel, 3, (sent,), "first_departure")(named, own_obs, own_var)
    copies = summed(send, place, hour_rows, ens_buf, tile_buf)
    partials, first_grad = next_forward(
        tile_block, place, tile_count, control, copies, hour_rows, bg_buf, ens_buf, tile_buf
    )
    received = exchange(partials, CELLS)
    final, send = depart(next_departure_kernel, 4, (own, sent), "next_departure")(
        named, received, own_obs, own_var
    )
    copies = summed(send, place, hour_rows, ens_buf, tile_buf)
    updated = control - step_size * first_grad
    second_grad = updated + jnp.sum(copies.astype(F32), axis=0)
    return jnp.stack([first_grad, second_grad]), final.reshape(1, receptors // devices)


def solution(mesh):
    torus = Mesh(
        mesh.devices.reshape(4, 4, 2, mesh.shape["rcpt"]), ("cells_0", "cells_1", "cells_2", "rcpt")
    )
    return jax.shard_map(
        per_device,
        mesh=torus,
        in_specs=(
            P(),
            P(None, CELLS),
            P(None, CELLS),
            P("rcpt", CELLS, None, None),
            P("rcpt", CELLS),
            P("rcpt", CELLS),
            P("rcpt", CELLS),
            P("rcpt", None),
            P("rcpt", None),
            P("rcpt", None),
        ),
        out_specs=(P(), P("rcpt", CELLS)),
        check_vma=False,
    )
```

```python
import jax
import jax.numpy as jnp
from jax import lax
from jax.experimental import pallas as pl
from jax.experimental.pallas import tpu as pltpu
from jax.sharding import Mesh
from jax.sharding import PartitionSpec as P

CELLS = ("cells_0", "cells_1", "cells_2")
PLANE = ("cells_0", "cells_1")
REST = ("cells_2", "rcpt")

step_size = 0.5

ENS_CHUNKS = 8
UNROLL = 32
NAMES = 8
F32 = jnp.float32
BF16 = jnp.bfloat16
I32 = jnp.int32


def slot_places(rows, share_tiles, per_share):
    slots = rows.shape[1]
    owner = jnp.broadcast_to(rows // share_tiles, (slots, slots))
    down = lax.broadcasted_iota(I32, (slots, slots), 0)
    across = lax.broadcasted_iota(I32, (slots, slots), 1)
    column = jnp.sum(jnp.where(down == across, owner, 0), axis=1, keepdims=True)
    earlier = (owner == column) & (down < across)
    rank = jnp.sum(earlier.astype(I32), axis=0, keepdims=True)
    return (rows // share_tiles) * per_share + rank


def emissions(scaled, background, ensemble, emis, c):
    blocks = ensemble.shape[2] // 128
    values = background[c] + jnp.dot(scaled, ensemble[c], preferred_element_type=F32)
    values = values.astype(BF16).astype(F32)
    for b in range(blocks):
        emis[c * blocks + b] = values[:, b * 128 : (b + 1) * 128]


def live_groups(live, work):
    lax.fori_loop(0, (live + UNROLL - 1) // UNROLL, lambda g, carry: (work(g), carry)[1], 0)


def split_halves(value):
    rounded = value.astype(BF16).astype(F32)
    return [rounded, value - rounded]


def forward_group(g, block, place, tiles, hour_rows, emis, partial):
    hours = emis.shape[1]
    hour_line = lax.broadcasted_iota(I32, (hours, 128), 0)
    none = jnp.zeros((hours, 128), F32)
    base = pl.multiple_of(g * UNROLL, UNROLL)
    these = hour_rows[pl.ds(base, UNROLL), :]
    for u in range(0, UNROLL, 2):
        s = base + u
        left = jnp.concatenate([emis[block[0, s]], none], axis=1)
        right = jnp.concatenate([none, emis[block[0, s + 1]]], axis=1)
        pair = jnp.concatenate([left, right], axis=0).astype(BF16)
        both = jnp.concatenate([tiles[s], tiles[s + 1]], axis=1)
        every = lax.dot_general(pair, both, (((1,), (1,)), ((), ())), preferred_element_type=F32)
        for v in range(2):
            chosen = hour_line == these[u + v : u + v + 1, :]
            part = jnp.where(chosen, every[v * hours : (v + 1) * hours], 0.0)
            partial[pl.ds(place[0, s + v], 1), :] = jnp.sum(part, axis=0, keepdims=True)


def first_forward_kernel(
    position, count, block_in, row_in, control, background, ensemble, footprint, hour,
    observed, inv_var,
    out, place_out, hour_rows, bg_buf, ens_buf, tile_buf, own_observed, own_inv_var,
    place, block, row, line_buf, control_buf, hour_buf, emis, partial, row_ids,
    ens_sem, bg_sem, tile_sem, hour_sem, place_sem, small_sem,
):
    slots = tile_buf.shape[0]
    width = ens_buf.shape[2]
    senders = out.shape[0]
    share_tiles = own_observed.shape[0]
    chunks = slots // UNROLL

    def ens_copy(c):
        return pltpu.make_async_copy(
            ensemble.at[:, pl.ds(c * width, width)], ens_buf.at[c], ens_sem.at[c]
        )

    def bg_copy(c):
        return pltpu.make_async_copy(
            background.at[:, pl.ds(c * width, width)], bg_buf.at[c], bg_sem.at[c]
        )

    def tile_copy(c):
        part = pl.ds(c * UNROLL, UNROLL)
        return pltpu.make_async_copy(footprint.at[part], tile_buf.at[part], tile_sem.at[c])

    share = pl.ds(position[0] * share_tiles, share_tiles)
    pairs = [
        (row_in, line_buf), (control, control_buf), (row_in, row),
        (block_in, block), (observed.at[share], own_observed), (inv_var.at[share], own_inv_var),
    ]
    small = [pltpu.make_async_copy(a, b, small_sem.at[i]) for i, (a, b) in enumerate(pairs)]
    for copy in small[:4]:
        copy.start()
    hour_copy = pltpu.make_async_copy(hour, hour_buf, hour_sem)
    hour_copy.start()
    for c in range(ENS_CHUNKS):
        ens_copy(c).start()
        bg_copy(c).start()

    small[0].wait()
    place_out[...] = slot_places(line_buf[...], share_tiles, slots // senders)
    place_copy = pltpu.make_async_copy(place_out, place, place_sem)
    place_copy.start()
    partial[...] = jnp.zeros_like(partial)
    row_ids[...] = jnp.zeros_like(row_ids)
    live = count[0, 0]
    small[1].wait()
    scaled = control_buf[...].astype(BF16)

    def start_tiles(c):
        @pl.when(c * UNROLL < live)
        def _():
            tile_copy(c).start()

    def name_slots(g, carry):
        for u in range(NAMES):
            s = g * NAMES + u
            here = row[0, s]
            shown = hour_buf[pl.ds(here, 1), :]
            hour_rows[pl.ds(s, 1), :] = jnp.where(s < live, shown, -1)
            number = (here & (share_tiles - 1)).astype(F32)
            row_ids[pl.ds(place[0, s], 1), :] = jnp.full((1, 128), number)
        return carry

    for c in range(ENS_CHUNKS):
        ens_copy(c).wait()
        bg_copy(c).wait()
        if c < chunks:
            start_tiles(c)
        emissions(scaled, bg_buf, ens_buf, emis, c)
        if c == 1:
            small[2].wait()
            place_copy.wait()
            hour_copy.wait()
            lax.fori_loop(0, ((live + UNROLL - 1) // UNROLL) * (UNROLL // NAMES), name_slots, 0)
    for c in range(ENS_CHUNKS, chunks):
        start_tiles(c)
    small[4].start()
    small[5].start()
    small[3].wait()

    def work(g):
        tile_copy(g).wait()
        forward_group(g, block, place, tile_buf, hour_rows, emis, partial)

    live_groups(live, work)
    small[4].wait()
    small[5].wait()
    parts = split_halves(partial[...]) + [row_ids[...]]
    parts = [part.reshape(senders, slots // senders, 128) for part in parts]
    out[...] = jnp.concatenate(parts, axis=1).astype(BF16)


def next_forward_kernel(
    block, place, count, control, copies, hour_rows, bg_buf, ens_buf, tile_buf,
    out, gradient, emis, partial,
):
    live = count[0, 0]
    slots = tile_buf.shape[0]
    senders = out.shape[0]
    total = control[...] + jnp.sum(copies[...], axis=0)
    gradient[...] = total
    scaled = (control[...] - step_size * total).astype(BF16)
    partial[...] = jnp.zeros_like(partial)
    for c in range(ENS_CHUNKS):
        emissions(scaled, bg_buf, ens_buf, emis, c)
    live_groups(live, lambda g: forward_group(g, block, place, tile_buf, hour_rows, emis, partial))
    parts = [part.reshape(senders, slots // senders, 128) for part in split_halves(partial[...])]
    out[...] = jnp.concatenate(parts, axis=1).astype(BF16)


def owner_pick(received, tiles):
    ids = received[...].astype(F32)[:, 16:24, 0:tiles].reshape(received.shape[0] * 8, tiles)
    lane = lax.broadcasted_iota(I32, ids.shape, 1).astype(F32)
    return jnp.where(ids == lane, 1.0, 0.0).astype(BF16)


def own_sum(pick, received):
    both = received[...].astype(F32)
    own = None
    for first in (0, 8):
        part = both[:, first : first + 8, :].reshape(pick.shape[0], 128).astype(BF16)
        part = lax.dot_general(pick, part, (((0,), (0,)), ((), ())), preferred_element_type=F32)
        own = part if own is None else own + part
    return own


def send_departure(pick, own, observed, inv_var, send):
    departure = (inv_var[...] * (own - observed[...])).astype(BF16)
    send[...] = jnp.dot(pick, departure, preferred_element_type=F32).astype(BF16)


def first_departure_kernel(received, observed, inv_var, send):
    pick = owner_pick(received, observed.shape[0])
    send_departure(pick, own_sum(pick, received), observed, inv_var, send)


def next_departure_kernel(named, received, observed, inv_var, modelled, send):
    pick = owner_pick(named, observed.shape[0])
    own = own_sum(pick, received)
    modelled[...] = own
    send_departure(pick, own, observed, inv_var, send)


def adjoint_kernel(
    block, place, count, departures, hour_rows, ens_buf, tile_buf, out, dep_buf, adjoint
):
    hours = out.shape[1]
    blocks = ens_buf.shape[2] // 128
    live = count[0, 0]
    hour_line = lax.broadcasted_iota(I32, (hours, 128), 0)
    dep_buf[...] = departures[...].astype(F32)
    adjoint[...] = jnp.zeros_like(adjoint)

    def work(g):
        base = pl.multiple_of(g * UNROLL, UNROLL)
        these = hour_rows[pl.ds(base, UNROLL), :]
        for u in range(0, UNROLL, 2):
            s = base + u
            weighted = []
            for v in range(2):
                chosen = hour_line == these[u + v : u + v + 1, :]
                weighted.append(jnp.where(chosen, dep_buf[pl.ds(place[0, s + v], 1), :], 0.0))
            pair = jnp.concatenate(weighted, axis=0).astype(BF16)
            both = jnp.concatenate([tile_buf[s], tile_buf[s + 1]], axis=1)
            every = jnp.dot(pair, both, preferred_element_type=F32)
            adjoint[block[0, s]] += every[0:hours, 0:128]
            adjoint[block[0, s + 1]] += every[hours : 2 * hours, 128:256]

    live_groups(live, work)
    total = jnp.zeros(out.shape[1:], F32)
    for c in range(ENS_CHUNKS):
        rounded = jnp.concatenate([adjoint[c * blocks + b] for b in range(blocks)], axis=1)
        total = total + lax.dot_general(
            rounded.astype(BF16), ens_buf[c], (((1,), (1,)), ((), ())), preferred_element_type=F32
        )
    total = total.astype(BF16)
    for j in range(out.shape[0]):
        out[j] = total


def last_adjoint_kernel(
    block, place, count, departures, hour_rows, ens_buf, tile_buf, own, out, final,
    dep_buf, adjoint, sem,
):
    copy = pltpu.make_async_copy(own, final, sem)
    copy.start()
    adjoint_kernel(
        block, place, count, departures, hour_rows, ens_buf, tile_buf, out, dep_buf, adjoint
    )
    copy.wait()


def sum_kernel(copies, out):
    total = jnp.sum(copies[...].astype(F32), axis=0)
    for j in range(out.shape[0]):
        out[j] = total


def exchange(value, axes):
    return lax.all_to_all(value, axes, 0, 0, tiled=True)


def per_device(
    control, background, ensemble, footprint, tile_block, tile_row, tile_count, hour, observed, inv_var,
):
    hours, members = control.shape
    cells_dev = background.shape[1]
    slots = footprint.shape[1]
    receptors = hour.shape[1]
    row_tiles = receptors // 128
    devices = lax.axis_size(CELLS)
    plane = lax.axis_size(PLANE)
    rest = lax.axis_size(REST)
    share_tiles = row_tiles // devices
    width = cells_dev // ENS_CHUNKS

    hour_tab = hour.reshape(row_tiles, 128)
    obs_tab = observed.reshape(row_tiles, 128)
    var_tab = inv_var.reshape(row_tiles, 128)
    position = lax.axis_index(CELLS).astype(I32).reshape(1)

    smem = pl.BlockSpec(memory_space=pltpu.SMEM)
    vmem = pl.BlockSpec(memory_space=pltpu.VMEM)
    hbm = pl.BlockSpec(memory_space=pl.ANY)
    limit = pltpu.CompilerParams(vmem_limit_bytes=24 * 1024 * 1024)
    emis = pltpu.VMEM((cells_dev // 128, hours, 128), F32)
    slot_lines = pltpu.VMEM((slots, 128), F32)

    first_forward = pl.pallas_call(
        first_forward_kernel,
        out_shape=(
            pltpu.VMEM((devices, 24, 128), BF16),
            pltpu.VMEM((1, slots), I32),
            pltpu.VMEM((slots, 128), I32),
            pltpu.VMEM((ENS_CHUNKS, hours, width), F32),
            pltpu.VMEM((ENS_CHUNKS, members, width), BF16),
            pltpu.VMEM((slots, 128, 128), BF16),
            pltpu.VMEM((share_tiles, 128), F32),
            pltpu.VMEM((share_tiles, 128), F32),
        ),
        in_specs=[smem, smem] + [hbm] * 9,
        out_specs=(vmem,) * 8,
        scratch_shapes=[
            pltpu.SMEM((1, slots), I32),
            pltpu.SMEM((1, slots), I32),
            pltpu.SMEM((1, slots), I32),
            pltpu.VMEM((1, slots), I32),
            pltpu.VMEM((hours, members), F32),
            pltpu.VMEM((row_tiles, 128), I32),
            emis,
            slot_lines,
            slot_lines,
            pltpu.SemaphoreType.DMA((ENS_CHUNKS,)),
            pltpu.SemaphoreType.DMA((ENS_CHUNKS,)),
            pltpu.SemaphoreType.DMA((slots // UNROLL,)),
            pltpu.SemaphoreType.DMA,
            pltpu.SemaphoreType.DMA,
            pltpu.SemaphoreType.DMA((6,)),
        ],
        compiler_params=limit,
        name="first_forward",
    )
    next_forward = pl.pallas_call(
        next_forward_kernel,
        out_shape=(
            pltpu.VMEM((devices, 16, 128), BF16),
            jax.ShapeDtypeStruct((hours, members), F32),
        ),
        in_specs=[smem, smem, smem] + [vmem] * 6,
        out_specs=(vmem, vmem),
        scratch_shapes=[emis, slot_lines],
        compiler_params=limit,
        name="next_forward",
    )

    sent = pltpu.VMEM((slots, 128), BF16)
    own = pltpu.VMEM((share_tiles, 128), F32)

    def depart(kernel, arrays, out_shape, name):
        return pl.pallas_call(
            kernel,
            out_shape=out_shape,
            in_specs=[vmem] * arrays,
            out_specs=(vmem,) * len(out_shape),
            compiler_params=pltpu.CompilerParams(vmem_limit_bytes=4 * 1024 * 1024),
            name=name,
        )

    adjoint = pl.pallas_call(
        adjoint_kernel,
        out_shape=pltpu.VMEM((rest, hours, members), BF16),
        in_specs=[smem, smem, smem] + [vmem] * 4,
        out_specs=vmem,
        scratch_shapes=[slot_lines, emis],
        compiler_params=limit,
        name="adjoint",
    )

    add_copies = pl.pallas_call(
        sum_kernel,
        out_shape=pltpu.VMEM((plane, hours, members), F32),
        in_specs=[vmem],
        out_specs=vmem,
        compiler_params=pltpu.CompilerParams(vmem_limit_bytes=4 * 1024 * 1024),
        name="add_copies",
    )

    last_adjoint = pl.pallas_call(
        last_adjoint_kernel,
        out_shape=(
            pltpu.VMEM((rest, hours, members), BF16),
            jax.ShapeDtypeStruct((share_tiles, 128), F32),
        ),
        in_specs=[smem, smem, smem] + [vmem] * 5,
        out_specs=(vmem, hbm),
        scratch_shapes=[slot_lines, emis, pltpu.SemaphoreType.DMA],
        compiler_params=limit,
        name="last_adjoint",
    )

    def sent_back(send):
        return exchange(send.reshape(devices, slots // devices, 128), CELLS).reshape(slots, 128)

    def summed(copies):
        return exchange(add_copies(exchange(copies, REST)), PLANE)

    pinned = [
        pltpu.with_memory_space_constraint(array, pltpu.HBM)
        for array in (
            tile_block, tile_row, control, background, ensemble, footprint[0],
            hour_tab, obs_tab, var_tab,
        )
    ]
    partials, place, hour_rows, bg_buf, ens_buf, tile_buf, own_obs, own_var = first_forward(
        position, tile_count, *pinned
    )
    named = exchange(partials, CELLS)
    (send,) = depart(first_departure_kernel, 3, (sent,), "first_departure")(named, own_obs, own_var)
    kept = (hour_rows, ens_buf, tile_buf)
    copies = summed(adjoint(tile_block, place, tile_count, sent_back(send), *kept))
    partials, first_grad = next_forward(
        tile_block, place, tile_count, control, copies, hour_rows, bg_buf, ens_buf, tile_buf
    )
    received = exchange(partials, CELLS)
    modelled, send = depart(next_departure_kernel, 4, (own, sent), "next_departure")(
        named, received, own_obs, own_var
    )
    copies, final = last_adjoint(
        tile_block, place, tile_count, sent_back(send), *kept, modelled
    )
    copies = summed(copies)
    updated = control - step_size * first_grad
    second_grad = updated + jnp.sum(copies, axis=0)
    return jnp.stack([first_grad, second_grad]), final.reshape(1, receptors // devices)


def solution(mesh):
    torus = Mesh(
        mesh.devices.reshape(4, 4, 2, mesh.shape["rcpt"]), ("cells_0", "cells_1", "cells_2", "rcpt")
    )
    return jax.shard_map(
        per_device,
        mesh=torus,
        in_specs=(
            P(),
            P(None, CELLS),
            P(None, CELLS),
            P("rcpt", CELLS, None, None),
            P("rcpt", CELLS),
            P("rcpt", CELLS),
            P("rcpt", CELLS),
            P("rcpt", None),
            P("rcpt", None),
            P("rcpt", None),
        ),
        out_specs=(P(), P("rcpt", CELLS)),
        check_vma=False,
    )
```

```python
import jax
import jax.numpy as jnp
from jax import lax
from jax.experimental import pallas as pl
from jax.experimental.pallas import tpu as pltpu
from jax.sharding import Mesh
from jax.sharding import PartitionSpec as P

CELLS = ("cells_0", "cells_1", "cells_2")
PLANE = ("cells_0", "cells_1")
REST = ("cells_2", "rcpt")

step_size = 0.5

ENS_CHUNKS = 8
TILE_CHUNK = 32
UNROLL = 64
NAMES = 8
F32 = jnp.float32
BF16 = jnp.bfloat16
I32 = jnp.int32


def slot_places(rows, share_tiles, per_share):
    slots = rows.shape[1]
    owner = jnp.broadcast_to(rows // share_tiles, (slots, slots))
    down = lax.broadcasted_iota(I32, (slots, slots), 0)
    across = lax.broadcasted_iota(I32, (slots, slots), 1)
    column = jnp.sum(jnp.where(down == across, owner, 0), axis=1, keepdims=True)
    earlier = (owner == column) & (down < across)
    rank = jnp.sum(earlier.astype(I32), axis=0, keepdims=True)
    return (rows // share_tiles) * per_share + rank


def emissions(scaled, background, ensemble, emis, c):
    blocks = ensemble.shape[2] // 128
    values = background[c] + jnp.dot(scaled, ensemble[c], preferred_element_type=F32)
    values = values.astype(BF16).astype(F32)
    for b in range(blocks):
        emis[c * blocks + b] = values[:, b * 128 : (b + 1) * 128]


def live_groups(live, unroll, work):
    lax.fori_loop(0, (live + unroll - 1) // unroll, lambda g, carry: (work(g), carry)[1], 0)


def forward_group(g, unroll, block, place, tiles, hour_rows, emis, partial):
    hours = emis.shape[1]
    hour_line = lax.broadcasted_iota(I32, (hours, 128), 0)
    none = jnp.zeros((hours, 128), F32)
    base = pl.multiple_of(g * unroll, unroll)
    these = hour_rows[pl.ds(base, unroll), :]
    for u in range(0, unroll, 2):
        s = base + u
        left = jnp.concatenate([emis[block[0, s]], none], axis=1)
        right = jnp.concatenate([none, emis[block[0, s + 1]]], axis=1)
        pair = jnp.concatenate([left, right], axis=0).astype(BF16)
        both = jnp.concatenate([tiles[s], tiles[s + 1]], axis=1)
        every = lax.dot_general(pair, both, (((1,), (1,)), ((), ())), preferred_element_type=F32)
        for v in range(2):
            chosen = hour_line == these[u + v : u + v + 1, :]
            part = jnp.where(chosen, every[v * hours : (v + 1) * hours], 0.0)
            partial[pl.ds(place[0, s + v], 1), :] = jnp.sum(part, axis=0, keepdims=True)


def first_forward_kernel(
    position, count, block_in, row_in, control, background, ensemble, footprint, hour,
    observed, inv_var,
    out, place_out, hour_rows, bg_buf, ens_buf, tile_buf, own_observed, own_inv_var,
    place, block, row, line_buf, control_buf, hour_buf, emis, partial, row_ids,
    ens_sem, bg_sem, tile_sem, hour_sem, place_sem, small_sem,
):
    slots = tile_buf.shape[0]
    width = ens_buf.shape[2]
    senders = out.shape[0]
    share_tiles = own_observed.shape[0]
    chunks = slots // TILE_CHUNK

    def ens_copy(c):
        return pltpu.make_async_copy(
            ensemble.at[:, pl.ds(c * width, width)], ens_buf.at[c], ens_sem.at[c]
        )

    def bg_copy(c):
        return pltpu.make_async_copy(
            background.at[:, pl.ds(c * width, width)], bg_buf.at[c], bg_sem.at[c]
        )

    def tile_copy(c):
        part = pl.ds(c * TILE_CHUNK, TILE_CHUNK)
        return pltpu.make_async_copy(footprint.at[part], tile_buf.at[part], tile_sem.at[c])

    share = pl.ds(position[0] * share_tiles, share_tiles)
    pairs = [
        (row_in, line_buf), (control, control_buf), (row_in, row),
        (block_in, block), (observed.at[share], own_observed), (inv_var.at[share], own_inv_var),
    ]
    small = [pltpu.make_async_copy(a, b, small_sem.at[i]) for i, (a, b) in enumerate(pairs)]
    for copy in small[:4]:
        copy.start()
    hour_copy = pltpu.make_async_copy(hour, hour_buf, hour_sem)
    hour_copy.start()
    for c in range(ENS_CHUNKS):
        ens_copy(c).start()
        bg_copy(c).start()

    small[0].wait()
    place_out[...] = slot_places(line_buf[...], share_tiles, slots // senders)
    place_copy = pltpu.make_async_copy(place_out, place, place_sem)
    place_copy.start()
    partial[...] = jnp.zeros_like(partial)
    row_ids[...] = jnp.zeros_like(row_ids)
    live = count[0, 0]
    filled = ((live + UNROLL - 1) // UNROLL) * UNROLL
    small[1].wait()
    scaled = control_buf[...].astype(BF16)

    def start_tiles(c):
        @pl.when(c * TILE_CHUNK < filled)
        def _():
            tile_copy(c).start()

    def name_slots(g, carry):
        for u in range(NAMES):
            s = g * NAMES + u
            here = row[0, s]
            shown = hour_buf[pl.ds(here, 1), :]
            hour_rows[pl.ds(s, 1), :] = jnp.where(s < live, shown, -1)
            number = (here & (share_tiles - 1)).astype(F32)
            row_ids[pl.ds(place[0, s], 1), :] = jnp.full((1, 128), number)
        return carry

    for c in range(ENS_CHUNKS):
        ens_copy(c).wait()
        bg_copy(c).wait()
        if c < chunks:
            start_tiles(c)
        emissions(scaled, bg_buf, ens_buf, emis, c)
        if c == 1:
            small[2].wait()
            place_copy.wait()
            hour_copy.wait()
            lax.fori_loop(0, filled // NAMES, name_slots, 0)
    for c in range(ENS_CHUNKS, chunks):
        start_tiles(c)
    small[4].start()
    small[5].start()
    small[3].wait()

    def work(g):
        tile_copy(g).wait()
        forward_group(g, TILE_CHUNK, block, place, tile_buf, hour_rows, emis, partial)

    live_groups(filled, TILE_CHUNK, work)
    small[4].wait()
    small[5].wait()
    parts = [part[...].reshape(senders, slots // senders, 128) for part in (partial, row_ids)]
    out[...] = jnp.concatenate(parts, axis=1).astype(BF16)


def next_forward_kernel(
    block, place, count, control, copies, hour_rows, bg_buf, ens_buf, tile_buf,
    out, gradient, emis, partial,
):
    live = count[0, 0]
    total = control[...] + jnp.sum(copies[...].astype(F32), axis=0)
    gradient[...] = total
    scaled = (control[...] - step_size * total).astype(BF16)
    partial[...] = jnp.zeros_like(partial)
    for c in range(ENS_CHUNKS):
        emissions(scaled, bg_buf, ens_buf, emis, c)
    live_groups(
        live, UNROLL,
        lambda g: forward_group(g, UNROLL, block, place, tile_buf, hour_rows, emis, partial),
    )
    out[...] = partial[...].astype(BF16)


def owner_pick(received, tiles):
    ids = received[...].astype(F32)[:, 8:16, 0:tiles].reshape(received.shape[0] * 8, tiles)
    lane = lax.broadcasted_iota(I32, ids.shape, 1).astype(F32)
    return jnp.where(ids == lane, 1.0, 0.0).astype(BF16)


def own_sum(pick, received):
    return lax.dot_general(pick, received, (((0,), (0,)), ((), ())), preferred_element_type=F32)


def send_departure(pick, own, observed, inv_var, send):
    departure = (inv_var[...] * (own - observed[...])).astype(BF16)
    send[...] = jnp.dot(pick, departure, preferred_element_type=F32).astype(BF16)


def first_departure_kernel(received, observed, inv_var, send):
    pick = owner_pick(received, observed.shape[0])
    data = received[...].astype(F32)[:, 0:8, :].reshape(pick.shape[0], 128).astype(BF16)
    send_departure(pick, own_sum(pick, data), observed, inv_var, send)


def next_departure_kernel(named, received, observed, inv_var, modelled, send):
    pick = owner_pick(named, observed.shape[0])
    own = own_sum(pick, received[...])
    modelled[...] = own
    send_departure(pick, own, observed, inv_var, send)


def adjoint_kernel(
    block, place, count, departures, hour_rows, ens_buf, tile_buf, out, dep_buf, adjoint
):
    hours = out.shape[1]
    blocks = ens_buf.shape[2] // 128
    live = count[0, 0]
    hour_line = lax.broadcasted_iota(I32, (hours, 128), 0)
    dep_buf[...] = departures[...].astype(F32)
    adjoint[...] = jnp.zeros_like(adjoint)

    def work(g):
        base = pl.multiple_of(g * UNROLL, UNROLL)
        these = hour_rows[pl.ds(base, UNROLL), :]
        for u in range(0, UNROLL, 2):
            s = base + u
            weighted = []
            for v in range(2):
                chosen = hour_line == these[u + v : u + v + 1, :]
                weighted.append(jnp.where(chosen, dep_buf[pl.ds(place[0, s + v], 1), :], 0.0))
            pair = jnp.concatenate(weighted, axis=0).astype(BF16)
            both = jnp.concatenate([tile_buf[s], tile_buf[s + 1]], axis=1)
            every = jnp.dot(pair, both, preferred_element_type=F32)
            adjoint[block[0, s]] += every[0:hours, 0:128]
            adjoint[block[0, s + 1]] += every[hours : 2 * hours, 128:256]

    live_groups(live, UNROLL, work)
    total = jnp.zeros((ens_buf.shape[1], hours), F32)
    for c in range(ENS_CHUNKS):
        rounded = jnp.concatenate([adjoint[c * blocks + b] for b in range(blocks)], axis=1)
        total = total + lax.dot_general(
            ens_buf[c], rounded.astype(BF16), (((1,), (1,)), ((), ())), preferred_element_type=F32
        )
    total = jnp.transpose(total)
    total = total.astype(BF16)
    for j in range(out.shape[0]):
        out[j] = total


def last_adjoint_kernel(
    block, place, count, departures, hour_rows, ens_buf, tile_buf, own, out, final,
    dep_buf, adjoint, sem,
):
    copy = pltpu.make_async_copy(own, final, sem)
    copy.start()
    adjoint_kernel(
        block, place, count, departures, hour_rows, ens_buf, tile_buf, out, dep_buf, adjoint
    )
    copy.wait()


def sum_kernel(copies, out):
    total = jnp.sum(copies[...].astype(F32), axis=0).astype(out.dtype)
    for j in range(out.shape[0]):
        out[j] = total


def exchange(value, axes):
    return lax.all_to_all(value, axes, 0, 0, tiled=True)


def per_device(
    control, background, ensemble, footprint, tile_block, tile_row, tile_count, hour, observed, inv_var,
):
    hours, members = control.shape
    cells_dev = background.shape[1]
    slots = footprint.shape[1]
    receptors = hour.shape[1]
    row_tiles = receptors // 128
    devices = lax.axis_size(CELLS)
    plane = lax.axis_size(PLANE)
    rest = lax.axis_size(REST)
    share_tiles = row_tiles // devices
    width = cells_dev // ENS_CHUNKS

    hour_tab = hour.reshape(row_tiles, 128)
    obs_tab = observed.reshape(row_tiles, 128)
    var_tab = inv_var.reshape(row_tiles, 128)
    position = lax.axis_index(CELLS).astype(I32).reshape(1)

    smem = pl.BlockSpec(memory_space=pltpu.SMEM)
    vmem = pl.BlockSpec(memory_space=pltpu.VMEM)
    hbm = pl.BlockSpec(memory_space=pl.ANY)
    limit = pltpu.CompilerParams(vmem_limit_bytes=24 * 1024 * 1024)
    emis = pltpu.VMEM((cells_dev // 128, hours, 128), F32)
    slot_lines = pltpu.VMEM((slots, 128), F32)

    first_forward = pl.pallas_call(
        first_forward_kernel,
        out_shape=(
            pltpu.VMEM((devices, 16, 128), BF16),
            pltpu.VMEM((1, slots), I32),
            pltpu.VMEM((slots, 128), I32),
            pltpu.VMEM((ENS_CHUNKS, hours, width), F32),
            pltpu.VMEM((ENS_CHUNKS, members, width), BF16),
            pltpu.VMEM((slots, 128, 128), BF16),
            pltpu.VMEM((share_tiles, 128), F32),
            pltpu.VMEM((share_tiles, 128), F32),
        ),
        in_specs=[smem, smem] + [hbm] * 9,
        out_specs=(vmem,) * 8,
        scratch_shapes=[
            pltpu.SMEM((1, slots), I32),
            pltpu.SMEM((1, slots), I32),
            pltpu.SMEM((1, slots), I32),
            pltpu.VMEM((1, slots), I32),
            pltpu.VMEM((hours, members), F32),
            pltpu.VMEM((row_tiles, 128), I32),
            emis,
            slot_lines,
            slot_lines,
            pltpu.SemaphoreType.DMA((ENS_CHUNKS,)),
            pltpu.SemaphoreType.DMA((ENS_CHUNKS,)),
            pltpu.SemaphoreType.DMA((slots // TILE_CHUNK,)),
            pltpu.SemaphoreType.DMA,
            pltpu.SemaphoreType.DMA,
            pltpu.SemaphoreType.DMA((6,)),
        ],
        compiler_params=limit,
        name="first_forward",
    )
    next_forward = pl.pallas_call(
        next_forward_kernel,
        out_shape=(
            pltpu.VMEM((slots, 128), BF16),
            jax.ShapeDtypeStruct((hours, members), F32),
        ),
        in_specs=[smem, smem, smem] + [vmem] * 6,
        out_specs=(vmem, vmem),
        scratch_shapes=[emis, slot_lines],
        compiler_params=limit,
        name="next_forward",
    )

    sent = pltpu.VMEM((slots, 128), BF16)
    own = pltpu.VMEM((share_tiles, 128), F32)

    def depart(kernel, arrays, out_shape, name):
        return pl.pallas_call(
            kernel,
            out_shape=out_shape,
            in_specs=[vmem] * arrays,
            out_specs=(vmem,) * len(out_shape),
            compiler_params=pltpu.CompilerParams(vmem_limit_bytes=4 * 1024 * 1024),
            name=name,
        )

    adjoint = pl.pallas_call(
        adjoint_kernel,
        out_shape=pltpu.VMEM((rest, hours, members), BF16),
        in_specs=[smem, smem, smem] + [vmem] * 4,
        out_specs=vmem,
        scratch_shapes=[slot_lines, emis],
        compiler_params=limit,
        name="adjoint",
    )

    def add_copies(copies, kind):
        return pl.pallas_call(
            sum_kernel,
            out_shape=pltpu.VMEM((plane, hours, members), kind),
            in_specs=[vmem],
            out_specs=vmem,
            compiler_params=pltpu.CompilerParams(vmem_limit_bytes=4 * 1024 * 1024),
            name="add_copies",
        )(copies)

    last_adjoint = pl.pallas_call(
        last_adjoint_kernel,
        out_shape=(
            pltpu.VMEM((rest, hours, members), BF16),
            jax.ShapeDtypeStruct((share_tiles, 128), F32),
        ),
        in_specs=[smem, smem, smem] + [vmem] * 5,
        out_specs=(vmem, hbm),
        scratch_shapes=[slot_lines, emis, pltpu.SemaphoreType.DMA],
        compiler_params=limit,
        name="last_adjoint",
    )

    def by_slots(rows):
        return exchange(rows.reshape(devices, slots // devices, 128), CELLS).reshape(slots, 128)

    def summed(copies, kind):
        return exchange(add_copies(exchange(copies, REST), kind), PLANE)

    pinned = [
        pltpu.with_memory_space_constraint(array, pltpu.HBM)
        for array in (
            tile_block, tile_row, control, background, ensemble, footprint[0],
            hour_tab, obs_tab, var_tab,
        )
    ]
    partials, place, hour_rows, bg_buf, ens_buf, tile_buf, own_obs, own_var = first_forward(
        position, tile_count, *pinned
    )
    named = exchange(partials, CELLS)
    (send,) = depart(first_departure_kernel, 3, (sent,), "first_departure")(named, own_obs, own_var)
    kept = (hour_rows, ens_buf, tile_buf)
    copies = summed(adjoint(tile_block, place, tile_count, by_slots(send), *kept), F32)
    partials, first_grad = next_forward(
        tile_block, place, tile_count, control, copies, hour_rows, bg_buf, ens_buf, tile_buf
    )
    received = by_slots(partials)
    modelled, send = depart(next_departure_kernel, 4, (own, sent), "next_departure")(
        named, received, own_obs, own_var
    )
    copies, final = last_adjoint(
        tile_block, place, tile_count, by_slots(send), *kept, modelled
    )
    copies = summed(copies, BF16)
    updated = control - step_size * first_grad
    second_grad = updated + jnp.sum(copies.astype(F32), axis=0)
    return jnp.stack([first_grad, second_grad]), final.reshape(1, receptors // devices)


def solution(mesh):
    torus = Mesh(
        mesh.devices.reshape(4, 4, 2, mesh.shape["rcpt"]), ("cells_0", "cells_1", "cells_2", "rcpt")
    )
    return jax.shard_map(
        per_device,
        mesh=torus,
        in_specs=(
            P(),
            P(None, CELLS),
            P(None, CELLS),
            P("rcpt", CELLS, None, None),
            P("rcpt", CELLS),
            P("rcpt", CELLS),
            P("rcpt", CELLS),
            P("rcpt", None),
            P("rcpt", None),
            P("rcpt", None),
        ),
        out_specs=(P(), P("rcpt", CELLS)),
        check_vma=False,
    )
```

```python
import jax
import jax.numpy as jnp
from jax import lax
from jax.experimental import pallas as pl
from jax.experimental.pallas import tpu as pltpu
from jax.sharding import Mesh
from jax.sharding import PartitionSpec as P

CELLS = ("cells_0", "cells_1", "cells_2")
PLANE = ("cells_0", "cells_1")
REST = ("cells_2", "rcpt")

step_size = 0.5

ENS_CHUNKS = 8
HOURS_AFTER = 2
TILES_AT_ONCE = 2
TILE_CHUNK = 32
UNROLL = 64
NAMES = 8
F32 = jnp.float32
BF16 = jnp.bfloat16
I32 = jnp.int32


def slot_places(rows, share_tiles, per_share):
    slots = rows.shape[1]
    owner = jnp.broadcast_to(rows // share_tiles, (slots, slots))
    down = lax.broadcasted_iota(I32, (slots, slots), 0)
    across = lax.broadcasted_iota(I32, (slots, slots), 1)
    column = jnp.sum(jnp.where(down == across, owner, 0), axis=1, keepdims=True)
    earlier = (owner == column) & (down < across)
    rank = jnp.sum(earlier.astype(I32), axis=0, keepdims=True)
    return (rows // share_tiles) * per_share + rank


def emissions(scaled, background, ensemble, emis, c):
    blocks = ensemble.shape[2] // 128
    values = background[c] + jnp.dot(scaled, ensemble[c], preferred_element_type=F32)
    for b in range(blocks):
        emis[c * blocks + b] = values[:, b * 128 : (b + 1) * 128]


def live_groups(live, unroll, work):
    lax.fori_loop(0, (live + unroll - 1) // unroll, lambda g, carry: (work(g), carry)[1], 0)


def forward_group(g, unroll, block, place, tiles, hour_rows, emis, partial):
    hours = emis.shape[1]
    hour_line = lax.broadcasted_iota(I32, (hours, 128), 0)
    none = jnp.zeros((hours, 128), F32)
    base = pl.multiple_of(g * unroll, unroll)
    these = hour_rows[pl.ds(base, unroll), :]
    for u in range(0, unroll, 2):
        s = base + u
        left = jnp.concatenate([emis[block[0, s]], none], axis=1)
        right = jnp.concatenate([none, emis[block[0, s + 1]]], axis=1)
        pair = jnp.concatenate([left, right], axis=0).astype(BF16)
        both = jnp.concatenate([tiles[s], tiles[s + 1]], axis=1)
        every = lax.dot_general(pair, both, (((1,), (1,)), ((), ())), preferred_element_type=F32)
        for v in range(2):
            chosen = hour_line == these[u + v : u + v + 1, :]
            part = jnp.where(chosen, every[v * hours : (v + 1) * hours], 0.0)
            partial[pl.ds(place[0, s + v], 1), :] = jnp.sum(part, axis=0, keepdims=True)


def first_forward_kernel(
    count, block_in, row_in, control, background, ensemble, footprint, hour,
    observed, inv_var,
    out, place_out, hour_rows, bg_buf, ens_buf, tile_buf, own_observed, own_inv_var,
    place, block, row, line_buf, control_buf, hour_buf, emis, partial, row_ids,
    ens_sem, bg_sem, tile_sem, hour_sem, place_sem, small_sem,
):
    slots = tile_buf.shape[0]
    width = ens_buf.shape[2]
    senders = out.shape[0]
    share_tiles = own_observed.shape[0]
    chunks = slots // TILE_CHUNK

    def ens_copy(c):
        return pltpu.make_async_copy(
            ensemble.at[:, pl.ds(c * width, width)], ens_buf.at[c], ens_sem.at[c]
        )

    def bg_copy(c):
        return pltpu.make_async_copy(
            background.at[:, pl.ds(c * width, width)], bg_buf.at[c], bg_sem.at[c]
        )

    def tile_copy(c):
        part = pl.ds(c * TILE_CHUNK, TILE_CHUNK)
        return pltpu.make_async_copy(footprint.at[part], tile_buf.at[part], tile_sem.at[c])

    share = pl.ds(lax.axis_index(CELLS) * share_tiles, share_tiles)
    pairs = [
        (row_in, line_buf), (control, control_buf), (row_in, row),
        (block_in, block), (observed.at[share], own_observed), (inv_var.at[share], own_inv_var),
    ]
    small = [pltpu.make_async_copy(a, b, small_sem.at[i]) for i, (a, b) in enumerate(pairs)]
    for copy in small[:4]:
        copy.start()
    hour_copy = pltpu.make_async_copy(hour, hour_buf, hour_sem)
    for c in range(ENS_CHUNKS):
        ens_copy(c).start()
        bg_copy(c).start()
        if c == HOURS_AFTER:
            hour_copy.start()

    small[0].wait()
    live = count[0, 0]
    places = slot_places(line_buf[...], share_tiles, slots // senders)
    place_out[...] = jnp.concatenate([places, jnp.full((1, 128), live)], axis=1)
    place_copy = pltpu.make_async_copy(place_out, place, place_sem)
    place_copy.start()
    partial[...] = jnp.zeros_like(partial)
    row_ids[...] = jnp.zeros_like(row_ids)
    filled = ((live + UNROLL - 1) // UNROLL) * UNROLL
    small[1].wait()
    scaled = control_buf[...].astype(BF16)

    def start_tiles(c):
        @pl.when(c * TILE_CHUNK < filled)
        def _():
            tile_copy(c).start()

    def name_slots(g, carry):
        for u in range(NAMES):
            s = g * NAMES + u
            here = row[0, s]
            shown = hour_buf[pl.ds(here, 1), :]
            hour_rows[pl.ds(s, 1), :] = jnp.where(s < live, shown, -1)
            number = (here & (share_tiles - 1)).astype(F32)
            row_ids[pl.ds(place[0, s], 1), :] = jnp.full((1, 128), number)
        return carry

    for c in range(ENS_CHUNKS):
        ens_copy(c).wait()
        bg_copy(c).wait()
        for t in range(chunks):
            if ENS_CHUNKS - 1 - (chunks - 1 - t) // TILES_AT_ONCE == c:
                start_tiles(t)
        emissions(scaled, bg_buf, ens_buf, emis, c)
        if c == HOURS_AFTER + 2:
            small[2].wait()
            place_copy.wait()
            hour_copy.wait()
            lax.fori_loop(0, filled // NAMES, name_slots, 0)
    small[4].start()
    small[5].start()
    small[3].wait()

    def work(g):
        for part in range(UNROLL // TILE_CHUNK):
            tile_copy(g * (UNROLL // TILE_CHUNK) + part).wait()
        forward_group(g, UNROLL, block, place, tile_buf, hour_rows, emis, partial)

    live_groups(live, UNROLL, work)
    small[4].wait()
    small[5].wait()
    parts = [part[...].reshape(senders, slots // senders, 128) for part in (partial, row_ids)]
    out[...] = jnp.concatenate(parts, axis=1).astype(BF16)


def next_forward_kernel(
    block, place, control, copies, hour_rows, bg_buf, ens_buf, tile_buf,
    out, gradient, emis, partial,
):
    live = place[0, tile_buf.shape[0]]
    total = control[...] + jnp.sum(copies[...].astype(F32), axis=0)
    gradient[...] = total
    scaled = (control[...] - step_size * total).astype(BF16)
    partial[...] = jnp.zeros_like(partial)
    for c in range(ENS_CHUNKS):
        emissions(scaled, bg_buf, ens_buf, emis, c)
    live_groups(
        live, UNROLL,
        lambda g: forward_group(g, UNROLL, block, place, tile_buf, hour_rows, emis, partial),
    )
    out[...] = partial[...].astype(BF16)


def owner_pick(received, tiles):
    ids = received[...].astype(F32)[:, 8:16, 0:tiles].reshape(received.shape[0] * 8, tiles)
    lane = lax.broadcasted_iota(I32, ids.shape, 1).astype(F32)
    return jnp.where(ids == lane, 1.0, 0.0).astype(BF16)


def own_sum(pick, received):
    return lax.dot_general(pick, received, (((0,), (0,)), ((), ())), preferred_element_type=F32)


def send_departure(pick, own, observed, inv_var, send):
    departure = (inv_var[...] * (own - observed[...])).astype(BF16)
    send[...] = jnp.dot(pick, departure, preferred_element_type=F32).astype(BF16)


def first_departure_kernel(received, observed, inv_var, send):
    pick = owner_pick(received, observed.shape[0])
    data = received[...].astype(F32)[:, 0:8, :].reshape(pick.shape[0], 128).astype(BF16)
    send_departure(pick, own_sum(pick, data), observed, inv_var, send)


def next_departure_kernel(named, received, observed, inv_var, modelled, send):
    pick = owner_pick(named, observed.shape[0])
    own = own_sum(pick, received[...])
    modelled[...] = own
    send_departure(pick, own, observed, inv_var, send)


def adjoint_kernel(
    block, place, departures, hour_rows, ens_buf, tile_buf, out, dep_buf, adjoint
):
    hours = out.shape[1]
    blocks = ens_buf.shape[2] // 128
    live = place[0, tile_buf.shape[0]]
    hour_line = lax.broadcasted_iota(I32, (hours, 128), 0)
    dep_buf[...] = departures[...].astype(F32)
    adjoint[...] = jnp.zeros_like(adjoint)

    def work(g):
        base = pl.multiple_of(g * UNROLL, UNROLL)
        these = hour_rows[pl.ds(base, UNROLL), :]
        for u in range(0, UNROLL, 2):
            s = base + u
            weighted = []
            for v in range(2):
                chosen = hour_line == these[u + v : u + v + 1, :]
                weighted.append(jnp.where(chosen, dep_buf[pl.ds(place[0, s + v], 1), :], 0.0))
            pair = jnp.concatenate(weighted, axis=0).astype(BF16)
            both = jnp.concatenate([tile_buf[s], tile_buf[s + 1]], axis=1)
            every = jnp.dot(pair, both, preferred_element_type=F32)
            adjoint[block[0, s]] += every[0:hours, 0:128]
            adjoint[block[0, s + 1]] += every[hours : 2 * hours, 128:256]

    live_groups(live, UNROLL, work)
    total = jnp.zeros((ens_buf.shape[1], hours), F32)
    for c in range(ENS_CHUNKS):
        rounded = jnp.concatenate([adjoint[c * blocks + b] for b in range(blocks)], axis=1)
        total = total + lax.dot_general(
            ens_buf[c], rounded.astype(BF16), (((1,), (1,)), ((), ())), preferred_element_type=F32
        )
    total = jnp.transpose(total)
    total = total.astype(BF16)
    for j in range(out.shape[0]):
        out[j] = total


def last_adjoint_kernel(
    block, place, departures, hour_rows, ens_buf, tile_buf, own, out, final,
    dep_buf, adjoint, sem,
):
    copy = pltpu.make_async_copy(own, final, sem)
    copy.start()
    adjoint_kernel(
        block, place, departures, hour_rows, ens_buf, tile_buf, out, dep_buf, adjoint
    )
    copy.wait()


def sum_kernel(copies, out):
    total = jnp.sum(copies[...].astype(F32), axis=0).astype(out.dtype)
    for j in range(out.shape[0]):
        out[j] = total


def exchange(value, axes):
    return lax.all_to_all(value, axes, 0, 0, tiled=True)


def per_device(
    control, background, ensemble, footprint, tile_block, tile_row, tile_count, hour, observed, inv_var,
):
    hours, members = control.shape
    cells_dev = background.shape[1]
    slots = footprint.shape[1]
    receptors = hour.shape[1]
    row_tiles = receptors // 128
    devices = lax.axis_size(CELLS)
    plane = lax.axis_size(PLANE)
    rest = lax.axis_size(REST)
    share_tiles = row_tiles // devices
    width = cells_dev // ENS_CHUNKS

    hour_tab = hour.reshape(row_tiles, 128)
    obs_tab = observed.reshape(row_tiles, 128)
    var_tab = inv_var.reshape(row_tiles, 128)

    smem = pl.BlockSpec(memory_space=pltpu.SMEM)
    vmem = pl.BlockSpec(memory_space=pltpu.VMEM)
    hbm = pl.BlockSpec(memory_space=pl.ANY)
    limit = pltpu.CompilerParams(vmem_limit_bytes=24 * 1024 * 1024)
    emis = pltpu.VMEM((cells_dev // 128, hours, 128), F32)
    slot_lines = pltpu.VMEM((slots, 128), F32)

    first_forward = pl.pallas_call(
        first_forward_kernel,
        out_shape=(
            pltpu.VMEM((devices, 16, 128), BF16),
            pltpu.VMEM((1, slots + 128), I32),
            pltpu.VMEM((slots, 128), I32),
            pltpu.VMEM((ENS_CHUNKS, hours, width), F32),
            pltpu.VMEM((ENS_CHUNKS, members, width), BF16),
            pltpu.VMEM((slots, 128, 128), BF16),
            pltpu.VMEM((share_tiles, 128), F32),
            pltpu.VMEM((share_tiles, 128), F32),
        ),
        in_specs=[smem] + [hbm] * 9,
        out_specs=(vmem,) * 8,
        scratch_shapes=[
            pltpu.SMEM((1, slots + 128), I32),
            pltpu.SMEM((1, slots), I32),
            pltpu.SMEM((1, slots), I32),
            pltpu.VMEM((1, slots), I32),
            pltpu.VMEM((hours, members), F32),
            pltpu.VMEM((row_tiles, 128), I32),
            emis,
            slot_lines,
            slot_lines,
            pltpu.SemaphoreType.DMA((ENS_CHUNKS,)),
            pltpu.SemaphoreType.DMA((ENS_CHUNKS,)),
            pltpu.SemaphoreType.DMA((slots // TILE_CHUNK,)),
            pltpu.SemaphoreType.DMA,
            pltpu.SemaphoreType.DMA,
            pltpu.SemaphoreType.DMA((6,)),
        ],
        compiler_params=limit,
        name="first_forward",
    )
    next_forward = pl.pallas_call(
        next_forward_kernel,
        out_shape=(
            pltpu.VMEM((slots, 128), BF16),
            jax.ShapeDtypeStruct((hours, members), F32),
        ),
        in_specs=[smem, smem] + [vmem] * 6,
        out_specs=(vmem, vmem),
        scratch_shapes=[emis, slot_lines],
        compiler_params=limit,
        name="next_forward",
    )

    sent = pltpu.VMEM((slots, 128), BF16)
    own = pltpu.VMEM((share_tiles, 128), F32)

    def depart(kernel, arrays, out_shape, name):
        return pl.pallas_call(
            kernel,
            out_shape=out_shape,
            in_specs=[vmem] * arrays,
            out_specs=(vmem,) * len(out_shape),
            compiler_params=pltpu.CompilerParams(vmem_limit_bytes=4 * 1024 * 1024),
            name=name,
        )

    adjoint = pl.pallas_call(
        adjoint_kernel,
        out_shape=pltpu.VMEM((plane, hours, members), BF16),
        in_specs=[smem, smem] + [vmem] * 4,
        out_specs=vmem,
        scratch_shapes=[slot_lines, emis],
        compiler_params=limit,
        name="adjoint",
    )

    def add_copies(copies, count, kind):
        return pl.pallas_call(
            sum_kernel,
            out_shape=pltpu.VMEM((count, hours, members), kind),
            in_specs=[vmem],
            out_specs=vmem,
            compiler_params=pltpu.CompilerParams(vmem_limit_bytes=4 * 1024 * 1024),
            name="add_copies",
        )(copies)

    last_adjoint = pl.pallas_call(
        last_adjoint_kernel,
        out_shape=(
            pltpu.VMEM((rest, hours, members), BF16),
            jax.ShapeDtypeStruct((share_tiles, 128), F32),
        ),
        in_specs=[smem, smem] + [vmem] * 5,
        out_specs=(vmem, hbm),
        scratch_shapes=[slot_lines, emis, pltpu.SemaphoreType.DMA],
        compiler_params=limit,
        name="last_adjoint",
    )

    def by_slots(rows):
        return exchange(rows.reshape(devices, slots // devices, 128), CELLS).reshape(slots, 128)

    pinned = [
        pltpu.with_memory_space_constraint(array, pltpu.HBM)
        for array in (
            tile_block, tile_row, control, background, ensemble, footprint[0],
            hour_tab, obs_tab, var_tab,
        )
    ]
    partials, place, hour_rows, bg_buf, ens_buf, tile_buf, own_obs, own_var = first_forward(
        tile_count, *pinned
    )
    named = exchange(partials, CELLS)
    (send,) = depart(first_departure_kernel, 3, (sent,), "first_departure")(named, own_obs, own_var)
    kept = (hour_rows, ens_buf, tile_buf)
    copies = adjoint(tile_block, place, by_slots(send), *kept)
    copies = exchange(add_copies(exchange(copies, PLANE), rest, F32), REST)
    partials, first_grad = next_forward(
        tile_block, place, control, copies, hour_rows, bg_buf, ens_buf, tile_buf
    )
    received = by_slots(partials)
    modelled, send = depart(next_departure_kernel, 4, (own, sent), "next_departure")(
        named, received, own_obs, own_var
    )
    copies, final = last_adjoint(
        tile_block, place, by_slots(send), *kept, modelled
    )
    copies = exchange(add_copies(exchange(copies, REST), plane, BF16), PLANE)
    updated = control - step_size * first_grad
    second_grad = updated + jnp.sum(copies.astype(F32), axis=0)
    return jnp.stack([first_grad, second_grad]), final.reshape(1, receptors // devices)


def solution(mesh):
    torus = Mesh(
        mesh.devices.reshape(4, 4, 2, mesh.shape["rcpt"]), ("cells_0", "cells_1", "cells_2", "rcpt")
    )
    return jax.shard_map(
        per_device,
        mesh=torus,
        in_specs=(
            P(),
            P(None, CELLS),
            P(None, CELLS),
            P("rcpt", CELLS, None, None),
            P("rcpt", CELLS),
            P("rcpt", CELLS),
            P("rcpt", CELLS),
            P("rcpt", None),
            P("rcpt", None),
            P("rcpt", None),
        ),
        out_specs=(P(), P("rcpt", CELLS)),
        check_vma=False,
    )
```

```python
import jax
import jax.numpy as jnp
from jax import lax
from jax.experimental import pallas as pl
from jax.experimental.pallas import tpu as pltpu
from jax.sharding import Mesh
from jax.sharding import PartitionSpec as P

CELLS = ("cells_0", "cells_1", "cells_2")
PLANE = ("cells_0", "cells_1")
REST = ("cells_2", "rcpt")

step_size = 0.5

ENS_CHUNKS = 8
HOURS_AFTER = 2
TILES_AT_ONCE = 2
TILE_CHUNK = 32
UNROLL = 64
NAMES = 8
F32 = jnp.float32
BF16 = jnp.bfloat16
I32 = jnp.int32


def slot_places(rows, share_tiles, per_share):
    slots = rows.shape[1]
    owner = jnp.broadcast_to(rows // share_tiles, (slots, slots))
    down = lax.broadcasted_iota(I32, (slots, slots), 0)
    across = lax.broadcasted_iota(I32, (slots, slots), 1)
    column = jnp.sum(jnp.where(down == across, owner, 0), axis=1, keepdims=True)
    earlier = (owner == column) & (down < across)
    rank = jnp.sum(earlier.astype(I32), axis=0, keepdims=True)
    return (rows // share_tiles) * per_share + rank


def emissions(scaled, background, ensemble, emis, c):
    blocks = ensemble.shape[2] // 128
    values = background[c] + jnp.dot(scaled, ensemble[c], preferred_element_type=F32)
    for b in range(blocks):
        emis[c * blocks + b] = values[:, b * 128 : (b + 1) * 128]


def live_groups(live, unroll, work):
    lax.fori_loop(0, (live + unroll - 1) // unroll, lambda g, carry: (work(g), carry)[1], 0)


def forward_group(g, unroll, block, place, tiles, hour_rows, emis, partial):
    hours = emis.shape[1]
    hour_line = lax.broadcasted_iota(I32, (hours, 128), 0)
    none = jnp.zeros((hours, 128), F32)
    base = pl.multiple_of(g * unroll, unroll)
    these = hour_rows[pl.ds(base, unroll), :]
    for u in range(0, unroll, 2):
        s = base + u
        left = jnp.concatenate([emis[block[0, s]], none], axis=1)
        right = jnp.concatenate([none, emis[block[0, s + 1]]], axis=1)
        pair = jnp.concatenate([left, right], axis=0).astype(BF16)
        both = jnp.concatenate([tiles[s], tiles[s + 1]], axis=1)
        every = lax.dot_general(pair, both, (((1,), (1,)), ((), ())), preferred_element_type=F32)
        for v in range(2):
            chosen = hour_line == these[u + v : u + v + 1, :]
            part = jnp.where(chosen, every[v * hours : (v + 1) * hours], 0.0)
            partial[pl.ds(place[0, s + v], 1), :] = jnp.sum(part, axis=0, keepdims=True)


def first_forward_kernel(
    count, block_in, row_in, control, background, ensemble, footprint, hour,
    observed, inv_var,
    out, place, block, hour_rows, bg_buf, ens_buf, tile_buf, own_observed, own_inv_var,
    place_buf, row, line_buf, control_buf, hour_buf, emis, partial, row_ids,
    ens_sem, bg_sem, tile_sem, hour_sem, place_sem, small_sem,
):
    slots = tile_buf.shape[0]
    width = ens_buf.shape[2]
    senders = out.shape[0]
    share_tiles = own_observed.shape[0]
    chunks = slots // TILE_CHUNK

    def ens_copy(c):
        return pltpu.make_async_copy(
            ensemble.at[:, pl.ds(c * width, width)], ens_buf.at[c], ens_sem.at[c]
        )

    def bg_copy(c):
        return pltpu.make_async_copy(
            background.at[:, pl.ds(c * width, width)], bg_buf.at[c], bg_sem.at[c]
        )

    def tile_copy(c):
        part = pl.ds(c * TILE_CHUNK, TILE_CHUNK)
        return pltpu.make_async_copy(footprint.at[part], tile_buf.at[part], tile_sem.at[c])

    share = pl.ds(lax.axis_index(CELLS) * share_tiles, share_tiles)
    pairs = [
        (row_in, line_buf), (control, control_buf), (row_in, row),
        (block_in, block), (observed.at[share], own_observed), (inv_var.at[share], own_inv_var),
    ]
    small = [pltpu.make_async_copy(a, b, small_sem.at[i]) for i, (a, b) in enumerate(pairs)]
    for copy in small[:4]:
        copy.start()
    hour_copy = pltpu.make_async_copy(hour, hour_buf, hour_sem)
    for c in range(ENS_CHUNKS):
        ens_copy(c).start()
        bg_copy(c).start()
        if c == HOURS_AFTER:
            hour_copy.start()

    small[0].wait()
    live = count[0, 0]
    places = slot_places(line_buf[...], share_tiles, slots // senders)
    place_buf[...] = jnp.concatenate([places, jnp.full((1, 128), live)], axis=1)
    place_copy = pltpu.make_async_copy(place_buf, place, place_sem)
    place_copy.start()
    partial[...] = jnp.zeros_like(partial)
    row_ids[...] = jnp.zeros_like(row_ids)
    filled = ((live + UNROLL - 1) // UNROLL) * UNROLL
    small[1].wait()
    scaled = control_buf[...].astype(BF16)

    def start_tiles(c):
        @pl.when(c * TILE_CHUNK < filled)
        def _():
            tile_copy(c).start()

    def name_slots(g, carry):
        for u in range(NAMES):
            s = g * NAMES + u
            here = row[0, s]
            shown = hour_buf[pl.ds(here, 1), :]
            hour_rows[pl.ds(s, 1), :] = jnp.where(s < live, shown, -1)
            number = (here & (share_tiles - 1)).astype(F32)
            row_ids[pl.ds(place[0, s], 1), :] = jnp.full((1, 128), number)
        return carry

    for c in range(ENS_CHUNKS):
        ens_copy(c).wait()
        bg_copy(c).wait()
        for t in range(chunks):
            if ENS_CHUNKS - 1 - (chunks - 1 - t) // TILES_AT_ONCE == c:
                start_tiles(t)
        emissions(scaled, bg_buf, ens_buf, emis, c)
        if c == HOURS_AFTER + 2:
            small[2].wait()
            place_copy.wait()
            hour_copy.wait()
            lax.fori_loop(0, filled // NAMES, name_slots, 0)
    small[4].start()
    small[5].start()
    small[3].wait()

    def work(g):
        for part in range(UNROLL // TILE_CHUNK):
            tile_copy(g * (UNROLL // TILE_CHUNK) + part).wait()
        forward_group(g, UNROLL, block, place, tile_buf, hour_rows, emis, partial)

    live_groups(live, UNROLL, work)
    small[4].wait()
    small[5].wait()
    parts = [part[...].reshape(senders, slots // senders, 128) for part in (partial, row_ids)]
    out[...] = jnp.concatenate(parts, axis=1).astype(BF16)


def next_forward_kernel(
    block, place, control, copies, hour_rows, bg_buf, ens_buf, tile_buf,
    out, gradient, emis, partial,
):
    live = place[0, tile_buf.shape[0]]
    total = control[...] + jnp.sum(copies[...].astype(F32), axis=0)
    gradient[...] = total
    scaled = (control[...] - step_size * total).astype(BF16)
    partial[...] = jnp.zeros_like(partial)
    for c in range(ENS_CHUNKS):
        emissions(scaled, bg_buf, ens_buf, emis, c)
    live_groups(
        live, UNROLL,
        lambda g: forward_group(g, UNROLL, block, place, tile_buf, hour_rows, emis, partial),
    )
    out[...] = partial[...].astype(BF16)


def owner_pick(received, tiles):
    ids = received[...].astype(F32)[:, 8:16, 0:tiles].reshape(received.shape[0] * 8, tiles)
    lane = lax.broadcasted_iota(I32, ids.shape, 1).astype(F32)
    return jnp.where(ids == lane, 1.0, 0.0).astype(BF16)


def own_sum(pick, received):
    return lax.dot_general(pick, received, (((0,), (0,)), ((), ())), preferred_element_type=F32)


def send_departure(pick, own, observed, inv_var, send):
    departure = (inv_var[...] * (own - observed[...])).astype(BF16)
    send[...] = jnp.dot(pick, departure, preferred_element_type=F32).astype(BF16)


def first_departure_kernel(received, observed, inv_var, send):
    pick = owner_pick(received, observed.shape[0])
    data = received[...].astype(F32)[:, 0:8, :].reshape(pick.shape[0], 128).astype(BF16)
    send_departure(pick, own_sum(pick, data), observed, inv_var, send)


def next_departure_kernel(named, received, observed, inv_var, modelled, send):
    pick = owner_pick(named, observed.shape[0])
    own = own_sum(pick, received[...])
    modelled[...] = own
    send_departure(pick, own, observed, inv_var, send)


def adjoint_kernel(
    block, place, departures, hour_rows, ens_buf, tile_buf, out, dep_buf, adjoint
):
    hours = out.shape[1]
    blocks = ens_buf.shape[2] // 128
    live = place[0, tile_buf.shape[0]]
    hour_line = lax.broadcasted_iota(I32, (hours, 128), 0)
    dep_buf[...] = departures[...].astype(F32)
    adjoint[...] = jnp.zeros_like(adjoint)

    def work(g):
        base = pl.multiple_of(g * UNROLL, UNROLL)
        these = hour_rows[pl.ds(base, UNROLL), :]
        for u in range(0, UNROLL, 2):
            s = base + u
            weighted = []
            for v in range(2):
                chosen = hour_line == these[u + v : u + v + 1, :]
                weighted.append(jnp.where(chosen, dep_buf[pl.ds(place[0, s + v], 1), :], 0.0))
            pair = jnp.concatenate(weighted, axis=0).astype(BF16)
            both = jnp.concatenate([tile_buf[s], tile_buf[s + 1]], axis=1)
            every = jnp.dot(pair, both, preferred_element_type=F32)
            adjoint[block[0, s]] += every[0:hours, 0:128]
            adjoint[block[0, s + 1]] += every[hours : 2 * hours, 128:256]

    live_groups(live, UNROLL, work)
    total = jnp.zeros((ens_buf.shape[1], hours), F32)
    for c in range(ENS_CHUNKS):
        rounded = jnp.concatenate([adjoint[c * blocks + b] for b in range(blocks)], axis=1)
        total = total + lax.dot_general(
            ens_buf[c], rounded.astype(BF16), (((1,), (1,)), ((), ())), preferred_element_type=F32
        )
    total = jnp.transpose(total)
    total = total.astype(BF16)
    for j in range(out.shape[0]):
        out[j] = total


def last_adjoint_kernel(
    block, place, departures, hour_rows, ens_buf, tile_buf, own, out, final,
    dep_buf, adjoint, sem,
):
    copy = pltpu.make_async_copy(own, final, sem)
    copy.start()
    adjoint_kernel(
        block, place, departures, hour_rows, ens_buf, tile_buf, out, dep_buf, adjoint
    )
    copy.wait()


def sum_kernel(copies, out):
    total = jnp.sum(copies[...].astype(F32), axis=0).astype(out.dtype)
    for j in range(out.shape[0]):
        out[j] = total


def exchange(value, axes):
    return lax.all_to_all(value, axes, 0, 0, tiled=True)


def per_device(
    control, background, ensemble, footprint, tile_block, tile_row, tile_count, hour, observed, inv_var,
):
    hours, members = control.shape
    cells_dev = background.shape[1]
    slots = footprint.shape[1]
    receptors = hour.shape[1]
    row_tiles = receptors // 128
    devices = lax.axis_size(CELLS)
    plane = lax.axis_size(PLANE)
    rest = lax.axis_size(REST)
    share_tiles = row_tiles // devices
    width = cells_dev // ENS_CHUNKS

    hour_tab = hour.reshape(row_tiles, 128)
    obs_tab = observed.reshape(row_tiles, 128)
    var_tab = inv_var.reshape(row_tiles, 128)

    smem = pl.BlockSpec(memory_space=pltpu.SMEM)
    vmem = pl.BlockSpec(memory_space=pltpu.VMEM)
    hbm = pl.BlockSpec(memory_space=pl.ANY)
    limit = pltpu.CompilerParams(vmem_limit_bytes=24 * 1024 * 1024)
    emis = pltpu.VMEM((cells_dev // 128, hours, 128), F32)
    slot_lines = pltpu.VMEM((slots, 128), F32)

    first_forward = pl.pallas_call(
        first_forward_kernel,
        out_shape=(
            pltpu.VMEM((devices, 16, 128), BF16),
            pltpu.SMEM((1, slots + 128), I32),
            pltpu.SMEM((1, slots), I32),
            pltpu.VMEM((slots, 128), I32),
            pltpu.VMEM((ENS_CHUNKS, hours, width), F32),
            pltpu.VMEM((ENS_CHUNKS, members, width), BF16),
            pltpu.VMEM((slots, 128, 128), BF16),
            pltpu.VMEM((share_tiles, 128), F32),
            pltpu.VMEM((share_tiles, 128), F32),
        ),
        in_specs=[smem] + [hbm] * 9,
        out_specs=(vmem, smem, smem) + (vmem,) * 6,
        scratch_shapes=[
            pltpu.VMEM((1, slots + 128), I32),
            pltpu.SMEM((1, slots), I32),
            pltpu.VMEM((1, slots), I32),
            pltpu.VMEM((hours, members), F32),
            pltpu.VMEM((row_tiles, 128), I32),
            emis,
            slot_lines,
            slot_lines,
            pltpu.SemaphoreType.DMA((ENS_CHUNKS,)),
            pltpu.SemaphoreType.DMA((ENS_CHUNKS,)),
            pltpu.SemaphoreType.DMA((slots // TILE_CHUNK,)),
            pltpu.SemaphoreType.DMA,
            pltpu.SemaphoreType.DMA,
            pltpu.SemaphoreType.DMA((6,)),
        ],
        compiler_params=limit,
        name="first_forward",
    )
    next_forward = pl.pallas_call(
        next_forward_kernel,
        out_shape=(
            pltpu.VMEM((slots, 128), BF16),
            jax.ShapeDtypeStruct((hours, members), F32),
        ),
        in_specs=[smem, smem] + [vmem] * 6,
        out_specs=(vmem, vmem),
        scratch_shapes=[emis, slot_lines],
        compiler_params=limit,
        name="next_forward",
    )

    sent = pltpu.VMEM((slots, 128), BF16)
    own = pltpu.VMEM((share_tiles, 128), F32)

    def depart(kernel, arrays, out_shape, name):
        return pl.pallas_call(
            kernel,
            out_shape=out_shape,
            in_specs=[vmem] * arrays,
            out_specs=(vmem,) * len(out_shape),
            compiler_params=pltpu.CompilerParams(vmem_limit_bytes=4 * 1024 * 1024),
            name=name,
        )

    adjoint = pl.pallas_call(
        adjoint_kernel,
        out_shape=pltpu.VMEM((plane, hours, members), BF16),
        in_specs=[smem, smem] + [vmem] * 4,
        out_specs=vmem,
        scratch_shapes=[slot_lines, emis],
        compiler_params=limit,
        name="adjoint",
    )

    def add_copies(copies, count, kind):
        return pl.pallas_call(
            sum_kernel,
            out_shape=pltpu.VMEM((count, hours, members), kind),
            in_specs=[vmem],
            out_specs=vmem,
            compiler_params=pltpu.CompilerParams(vmem_limit_bytes=4 * 1024 * 1024),
            name="add_copies",
        )(copies)

    last_adjoint = pl.pallas_call(
        last_adjoint_kernel,
        out_shape=(
            pltpu.VMEM((rest, hours, members), BF16),
            jax.ShapeDtypeStruct((share_tiles, 128), F32),
        ),
        in_specs=[smem, smem] + [vmem] * 5,
        out_specs=(vmem, hbm),
        scratch_shapes=[slot_lines, emis, pltpu.SemaphoreType.DMA],
        compiler_params=limit,
        name="last_adjoint",
    )

    def by_slots(rows):
        return exchange(rows.reshape(devices, slots // devices, 128), CELLS).reshape(slots, 128)

    pinned = [
        pltpu.with_memory_space_constraint(array, pltpu.HBM)
        for array in (
            tile_block, tile_row, control, background, ensemble, footprint[0],
            hour_tab, obs_tab, var_tab,
        )
    ]
    partials, place, block, hour_rows, bg_buf, ens_buf, tile_buf, own_obs, own_var = first_forward(
        tile_count, *pinned
    )
    named = exchange(partials, CELLS)
    (send,) = depart(first_departure_kernel, 3, (sent,), "first_departure")(named, own_obs, own_var)
    kept = (hour_rows, ens_buf, tile_buf)
    copies = adjoint(block, place, by_slots(send), *kept)
    copies = exchange(add_copies(exchange(copies, PLANE), rest, F32), REST)
    partials, first_grad = next_forward(
        block, place, control, copies, hour_rows, bg_buf, ens_buf, tile_buf
    )
    received = by_slots(partials)
    modelled, send = depart(next_departure_kernel, 4, (own, sent), "next_departure")(
        named, received, own_obs, own_var
    )
    copies, final = last_adjoint(
        block, place, by_slots(send), *kept, modelled
    )
    copies = exchange(add_copies(exchange(copies, REST), plane, BF16), PLANE)
    updated = control - step_size * first_grad
    second_grad = updated + jnp.sum(copies.astype(F32), axis=0)
    return jnp.stack([first_grad, second_grad]), final.reshape(1, receptors // devices)


def solution(mesh):
    torus = Mesh(
        mesh.devices.reshape(4, 4, 2, mesh.shape["rcpt"]), ("cells_0", "cells_1", "cells_2", "rcpt")
    )
    return jax.shard_map(
        per_device,
        mesh=torus,
        in_specs=(
            P(),
            P(None, CELLS),
            P(None, CELLS),
            P("rcpt", CELLS, None, None),
            P("rcpt", CELLS),
            P("rcpt", CELLS),
            P("rcpt", CELLS),
            P("rcpt", None),
            P("rcpt", None),
            P("rcpt", None),
        ),
        out_specs=(P(), P("rcpt", CELLS)),
        check_vma=False,
    )
```

```python
import jax
import jax.numpy as jnp
from jax import lax
from jax.experimental import pallas as pl
from jax.experimental.pallas import tpu as pltpu
from jax.sharding import Mesh
from jax.sharding import PartitionSpec as P

CELLS = ("cells_0", "cells_1", "cells_2")
PLANE = ("cells_0", "cells_1")
REST = ("cells_2", "rcpt")

step_size = 0.5

ENS_CHUNKS = 8
HOURS_AFTER = 2
TILES_AT_ONCE = 2
TILE_CHUNK = 32
FIRST_UNROLL = 64
UNROLL = 128
NAMES = 8
F32 = jnp.float32
BF16 = jnp.bfloat16
I32 = jnp.int32


def slot_places(rows, share_tiles, per_share):
    slots = rows.shape[1]
    owner = jnp.broadcast_to(rows // share_tiles, (slots, slots))
    down = lax.broadcasted_iota(I32, (slots, slots), 0)
    across = lax.broadcasted_iota(I32, (slots, slots), 1)
    column = jnp.sum(jnp.where(down == across, owner, 0), axis=1, keepdims=True)
    earlier = (owner == column) & (down < across)
    rank = jnp.sum(earlier.astype(I32), axis=0, keepdims=True)
    return (rows // share_tiles) * per_share + rank


def emissions(scaled, background, ensemble, emis, c):
    blocks = ensemble.shape[2] // 128
    values = background[c] + jnp.dot(scaled, ensemble[c], preferred_element_type=F32)
    for b in range(blocks):
        emis[c * blocks + b] = values[:, b * 128 : (b + 1) * 128]


def live_groups(live, unroll, work):
    lax.fori_loop(0, (live + unroll - 1) // unroll, lambda g, carry: (work(g), carry)[1], 0)


def forward_group(g, unroll, block, place, tiles, hour_rows, emis, partial):
    hours = emis.shape[1]
    hour_line = lax.broadcasted_iota(I32, (hours, 128), 0)
    none = jnp.zeros((hours, 128), F32)
    base = pl.multiple_of(g * unroll, unroll)
    these = hour_rows[pl.ds(base, unroll), :]
    for u in range(0, unroll, 2):
        s = base + u
        left = jnp.concatenate([emis[block[0, s]], none], axis=1)
        right = jnp.concatenate([none, emis[block[0, s + 1]]], axis=1)
        pair = jnp.concatenate([left, right], axis=0).astype(BF16)
        both = jnp.concatenate([tiles[s], tiles[s + 1]], axis=1)
        every = lax.dot_general(pair, both, (((1,), (1,)), ((), ())), preferred_element_type=F32)
        for v in range(2):
            chosen = hour_line == these[u + v : u + v + 1, :]
            part = jnp.where(chosen, every[v * hours : (v + 1) * hours], 0.0)
            partial[pl.ds(place[0, s + v], 1), :] = jnp.sum(part, axis=0, keepdims=True)


def first_forward_kernel(
    count, block_in, row_in, control, background, ensemble, footprint, hour,
    observed, inv_var,
    out, place, block, hour_rows, bg_buf, ens_buf, tile_buf, own_observed, own_inv_var,
    place_buf, row, line_buf, control_buf, hour_buf, emis, partial, row_ids,
    ens_sem, bg_sem, tile_sem, hour_sem, place_sem, small_sem,
):
    slots = tile_buf.shape[0]
    width = ens_buf.shape[2]
    senders = out.shape[0]
    share_tiles = own_observed.shape[0]
    chunks = slots // TILE_CHUNK

    def ens_copy(c):
        return pltpu.make_async_copy(
            ensemble.at[:, pl.ds(c * width, width)], ens_buf.at[c], ens_sem.at[c]
        )

    def bg_copy(c):
        return pltpu.make_async_copy(
            background.at[:, pl.ds(c * width, width)], bg_buf.at[c], bg_sem.at[c]
        )

    def tile_copy(c):
        part = pl.ds(c * TILE_CHUNK, TILE_CHUNK)
        return pltpu.make_async_copy(footprint.at[part], tile_buf.at[part], tile_sem.at[c])

    share = pl.ds(lax.axis_index(CELLS) * share_tiles, share_tiles)
    pairs = [
        (row_in, line_buf), (control, control_buf), (row_in, row),
        (block_in, block), (observed.at[share], own_observed), (inv_var.at[share], own_inv_var),
    ]
    small = [pltpu.make_async_copy(a, b, small_sem.at[i]) for i, (a, b) in enumerate(pairs)]
    for copy in small[:4]:
        copy.start()
    hour_copy = pltpu.make_async_copy(hour, hour_buf, hour_sem)
    for c in range(ENS_CHUNKS):
        ens_copy(c).start()
        bg_copy(c).start()
        if c == HOURS_AFTER:
            hour_copy.start()

    small[0].wait()
    live = count[0, 0]
    places = slot_places(line_buf[...], share_tiles, slots // senders)
    place_buf[...] = jnp.concatenate([places, jnp.full((1, 128), live)], axis=1)
    place_copy = pltpu.make_async_copy(place_buf, place, place_sem)
    place_copy.start()
    partial[...] = jnp.zeros_like(partial)
    row_ids[...] = jnp.zeros_like(row_ids)
    filled = ((live + UNROLL - 1) // UNROLL) * UNROLL
    small[1].wait()
    scaled = control_buf[...].astype(BF16)

    def start_tiles(c):
        @pl.when(c * TILE_CHUNK < filled)
        def _():
            tile_copy(c).start()

    def name_slots(g, carry):
        for u in range(NAMES):
            s = g * NAMES + u
            here = row[0, s]
            shown = hour_buf[pl.ds(here, 1), :]
            hour_rows[pl.ds(s, 1), :] = jnp.where(s < live, shown, -1)
            number = (here & (share_tiles - 1)).astype(F32)
            row_ids[pl.ds(place[0, s], 1), :] = jnp.full((1, 128), number)
        return carry

    for c in range(ENS_CHUNKS):
        ens_copy(c).wait()
        bg_copy(c).wait()
        for t in range(chunks):
            if ENS_CHUNKS - 1 - (chunks - 1 - t) // TILES_AT_ONCE == c:
                start_tiles(t)
        emissions(scaled, bg_buf, ens_buf, emis, c)
        if c == HOURS_AFTER + 2:
            small[2].wait()
            place_copy.wait()
            hour_copy.wait()
            lax.fori_loop(0, filled // NAMES, name_slots, 0)
    small[4].start()
    small[5].start()
    small[3].wait()

    def work(g):
        for part in range(FIRST_UNROLL // TILE_CHUNK):
            tile_copy(g * (FIRST_UNROLL // TILE_CHUNK) + part).wait()
        forward_group(g, FIRST_UNROLL, block, place, tile_buf, hour_rows, emis, partial)

    live_groups(live, FIRST_UNROLL, work)
    taken = ((live + FIRST_UNROLL - 1) // FIRST_UNROLL) * FIRST_UNROLL
    for c in range(chunks):
        @pl.when((c * TILE_CHUNK >= taken) & (c * TILE_CHUNK < filled))
        def _():
            tile_copy(c).wait()

    small[4].wait()
    small[5].wait()
    parts = [part[...].reshape(senders, slots // senders, 128) for part in (partial, row_ids)]
    out[...] = jnp.concatenate(parts, axis=1).astype(BF16)


def next_forward_kernel(
    block, place, control, copies, hour_rows, bg_buf, ens_buf, tile_buf,
    out, gradient, emis, partial,
):
    live = place[0, tile_buf.shape[0]]
    total = control[...] + jnp.sum(copies[...].astype(F32), axis=0)
    gradient[...] = total
    scaled = (control[...] - step_size * total).astype(BF16)
    partial[...] = jnp.zeros_like(partial)
    for c in range(ENS_CHUNKS):
        emissions(scaled, bg_buf, ens_buf, emis, c)
    live_groups(
        live, UNROLL,
        lambda g: forward_group(g, UNROLL, block, place, tile_buf, hour_rows, emis, partial),
    )
    out[...] = partial[...].astype(BF16)


def owner_pick(received, tiles):
    ids = received[...].astype(F32)[:, 8:16, 0:tiles].reshape(received.shape[0] * 8, tiles)
    lane = lax.broadcasted_iota(I32, ids.shape, 1).astype(F32)
    return jnp.where(ids == lane, 1.0, 0.0).astype(BF16)


def own_sum(pick, received):
    return lax.dot_general(pick, received, (((0,), (0,)), ((), ())), preferred_element_type=F32)


def send_departure(pick, own, observed, inv_var, send):
    departure = (inv_var[...] * (own - observed[...])).astype(BF16)
    send[...] = jnp.dot(pick, departure, preferred_element_type=F32).astype(BF16)


def first_departure_kernel(received, observed, inv_var, send):
    pick = owner_pick(received, observed.shape[0])
    data = received[...].astype(F32)[:, 0:8, :].reshape(pick.shape[0], 128).astype(BF16)
    send_departure(pick, own_sum(pick, data), observed, inv_var, send)


def next_departure_kernel(named, received, observed, inv_var, modelled, send):
    pick = owner_pick(named, observed.shape[0])
    own = own_sum(pick, received[...])
    modelled[...] = own
    send_departure(pick, own, observed, inv_var, send)


def adjoint_kernel(
    block, place, departures, hour_rows, ens_buf, tile_buf, out, dep_buf, adjoint
):
    hours = out.shape[1]
    blocks = ens_buf.shape[2] // 128
    live = place[0, tile_buf.shape[0]]
    hour_line = lax.broadcasted_iota(I32, (hours, 128), 0)
    dep_buf[...] = departures[...].astype(F32)
    adjoint[...] = jnp.zeros_like(adjoint)

    def work(g):
        base = pl.multiple_of(g * UNROLL, UNROLL)
        these = hour_rows[pl.ds(base, UNROLL), :]
        for u in range(0, UNROLL, 2):
            s = base + u
            weighted = []
            for v in range(2):
                chosen = hour_line == these[u + v : u + v + 1, :]
                weighted.append(jnp.where(chosen, dep_buf[pl.ds(place[0, s + v], 1), :], 0.0))
            pair = jnp.concatenate(weighted, axis=0).astype(BF16)
            both = jnp.concatenate([tile_buf[s], tile_buf[s + 1]], axis=1)
            every = jnp.dot(pair, both, preferred_element_type=F32)
            adjoint[block[0, s]] += every[0:hours, 0:128]
            adjoint[block[0, s + 1]] += every[hours : 2 * hours, 128:256]

    live_groups(live, UNROLL, work)
    total = jnp.zeros((ens_buf.shape[1], hours), F32)
    for c in range(ENS_CHUNKS):
        rounded = jnp.concatenate([adjoint[c * blocks + b] for b in range(blocks)], axis=1)
        total = total + lax.dot_general(
            ens_buf[c], rounded.astype(BF16), (((1,), (1,)), ((), ())), preferred_element_type=F32
        )
    total = jnp.transpose(total)
    total = total.astype(BF16)
    for j in range(out.shape[0]):
        out[j] = total


def last_adjoint_kernel(
    block, place, departures, hour_rows, ens_buf, tile_buf, own, out, final,
    dep_buf, adjoint, sem,
):
    copy = pltpu.make_async_copy(own, final, sem)
    copy.start()
    adjoint_kernel(
        block, place, departures, hour_rows, ens_buf, tile_buf, out, dep_buf, adjoint
    )
    copy.wait()


def sum_kernel(copies, out):
    total = jnp.sum(copies[...].astype(F32), axis=0).astype(out.dtype)
    for j in range(out.shape[0]):
        out[j] = total


def exchange(value, axes):
    return lax.all_to_all(value, axes, 0, 0, tiled=True)


def per_device(
    control, background, ensemble, footprint, tile_block, tile_row, tile_count, hour, observed, inv_var,
):
    hours, members = control.shape
    cells_dev = background.shape[1]
    slots = footprint.shape[1]
    receptors = hour.shape[1]
    row_tiles = receptors // 128
    devices = lax.axis_size(CELLS)
    plane = lax.axis_size(PLANE)
    rest = lax.axis_size(REST)
    share_tiles = row_tiles // devices
    width = cells_dev // ENS_CHUNKS

    hour_tab = hour.reshape(row_tiles, 128)
    obs_tab = observed.reshape(row_tiles, 128)
    var_tab = inv_var.reshape(row_tiles, 128)

    smem = pl.BlockSpec(memory_space=pltpu.SMEM)
    vmem = pl.BlockSpec(memory_space=pltpu.VMEM)
    hbm = pl.BlockSpec(memory_space=pl.ANY)
    limit = pltpu.CompilerParams(vmem_limit_bytes=24 * 1024 * 1024)
    emis = pltpu.VMEM((cells_dev // 128, hours, 128), F32)
    slot_lines = pltpu.VMEM((slots, 128), F32)

    first_forward = pl.pallas_call(
        first_forward_kernel,
        out_shape=(
            pltpu.VMEM((devices, 16, 128), BF16),
            pltpu.SMEM((1, slots + 128), I32),
            pltpu.SMEM((1, slots), I32),
            pltpu.VMEM((slots, 128), I32),
            pltpu.VMEM((ENS_CHUNKS, hours, width), F32),
            pltpu.VMEM((ENS_CHUNKS, members, width), BF16),
            pltpu.VMEM((slots, 128, 128), BF16),
            pltpu.VMEM((share_tiles, 128), F32),
            pltpu.VMEM((share_tiles, 128), F32),
        ),
        in_specs=[smem] + [hbm] * 9,
        out_specs=(vmem, smem, smem) + (vmem,) * 6,
        scratch_shapes=[
            pltpu.VMEM((1, slots + 128), I32),
            pltpu.SMEM((1, slots), I32),
            pltpu.VMEM((1, slots), I32),
            pltpu.VMEM((hours, members), F32),
            pltpu.VMEM((row_tiles, 128), I32),
            emis,
            slot_lines,
            slot_lines,
            pltpu.SemaphoreType.DMA((ENS_CHUNKS,)),
            pltpu.SemaphoreType.DMA((ENS_CHUNKS,)),
            pltpu.SemaphoreType.DMA((slots // TILE_CHUNK,)),
            pltpu.SemaphoreType.DMA,
            pltpu.SemaphoreType.DMA,
            pltpu.SemaphoreType.DMA((6,)),
        ],
        compiler_params=limit,
        name="first_forward",
    )
    next_forward = pl.pallas_call(
        next_forward_kernel,
        out_shape=(
            pltpu.VMEM((slots, 128), BF16),
            jax.ShapeDtypeStruct((hours, members), F32),
        ),
        in_specs=[smem, smem] + [vmem] * 6,
        out_specs=(vmem, vmem),
        scratch_shapes=[emis, slot_lines],
        compiler_params=limit,
        name="next_forward",
    )

    sent = pltpu.VMEM((slots, 128), BF16)
    own = pltpu.VMEM((share_tiles, 128), F32)

    def depart(kernel, arrays, out_shape, name):
        return pl.pallas_call(
            kernel,
            out_shape=out_shape,
            in_specs=[vmem] * arrays,
            out_specs=(vmem,) * len(out_shape),
            compiler_params=pltpu.CompilerParams(vmem_limit_bytes=4 * 1024 * 1024),
            name=name,
        )

    adjoint = pl.pallas_call(
        adjoint_kernel,
        out_shape=pltpu.VMEM((plane, hours, members), BF16),
        in_specs=[smem, smem] + [vmem] * 4,
        out_specs=vmem,
        scratch_shapes=[slot_lines, emis],
        compiler_params=limit,
        name="adjoint",
    )

    def add_copies(copies, count, kind):
        return pl.pallas_call(
            sum_kernel,
            out_shape=pltpu.VMEM((count, hours, members), kind),
            in_specs=[vmem],
            out_specs=vmem,
            compiler_params=pltpu.CompilerParams(vmem_limit_bytes=4 * 1024 * 1024),
            name="add_copies",
        )(copies)

    last_adjoint = pl.pallas_call(
        last_adjoint_kernel,
        out_shape=(
            pltpu.VMEM((rest, hours, members), BF16),
            jax.ShapeDtypeStruct((share_tiles, 128), F32),
        ),
        in_specs=[smem, smem] + [vmem] * 5,
        out_specs=(vmem, hbm),
        scratch_shapes=[slot_lines, emis, pltpu.SemaphoreType.DMA],
        compiler_params=limit,
        name="last_adjoint",
    )

    def by_slots(rows):
        return exchange(rows.reshape(devices, slots // devices, 128), CELLS).reshape(slots, 128)

    pinned = [
        pltpu.with_memory_space_constraint(array, pltpu.HBM)
        for array in (
            tile_block, tile_row, control, background, ensemble, footprint[0],
            hour_tab, obs_tab, var_tab,
        )
    ]
    partials, place, block, hour_rows, bg_buf, ens_buf, tile_buf, own_obs, own_var = first_forward(
        tile_count, *pinned
    )
    named = exchange(partials, CELLS)
    (send,) = depart(first_departure_kernel, 3, (sent,), "first_departure")(named, own_obs, own_var)
    kept = (hour_rows, ens_buf, tile_buf)
    copies = adjoint(block, place, by_slots(send), *kept)
    copies = exchange(add_copies(exchange(copies, PLANE), rest, F32), REST)
    partials, first_grad = next_forward(
        block, place, control, copies, hour_rows, bg_buf, ens_buf, tile_buf
    )
    received = by_slots(partials)
    modelled, send = depart(next_departure_kernel, 4, (own, sent), "next_departure")(
        named, received, own_obs, own_var
    )
    copies, final = last_adjoint(
        block, place, by_slots(send), *kept, modelled
    )
    copies = exchange(add_copies(exchange(copies, REST), plane, BF16), PLANE)
    updated = control - step_size * first_grad
    second_grad = updated + jnp.sum(copies.astype(F32), axis=0)
    return jnp.stack([first_grad, second_grad]), final.reshape(1, receptors // devices)


def solution(mesh):
    torus = Mesh(
        mesh.devices.reshape(4, 4, 2, mesh.shape["rcpt"]), ("cells_0", "cells_1", "cells_2", "rcpt")
    )
    return jax.shard_map(
        per_device,
        mesh=torus,
        in_specs=(
            P(),
            P(None, CELLS),
            P(None, CELLS),
            P("rcpt", CELLS, None, None),
            P("rcpt", CELLS),
            P("rcpt", CELLS),
            P("rcpt", CELLS),
            P("rcpt", None),
            P("rcpt", None),
            P("rcpt", None),
        ),
        out_specs=(P(), P("rcpt", CELLS)),
        check_vma=False,
    )
```

```python
import jax
import jax.numpy as jnp
from jax import lax
from jax.experimental import pallas as pl
from jax.experimental.pallas import tpu as pltpu
from jax.sharding import Mesh
from jax.sharding import PartitionSpec as P

CELLS = ("cells_0", "cells_1", "cells_2")
PLANE = ("cells_0", "cells_1")
REST = ("cells_2", "rcpt")

step_size = 0.5

ENS_CHUNKS = 8
HOURS_AFTER = 2
TILES_AT_ONCE = 2
TILE_CHUNK = 32
FIRST_UNROLL = 64
UNROLL = 128
NAMES = 8
F32 = jnp.float32
BF16 = jnp.bfloat16
I32 = jnp.int32


def slot_places(rows, share_tiles, per_share):
    slots = rows.shape[1]
    owner = jnp.broadcast_to(rows // share_tiles, (slots, slots))
    down = lax.broadcasted_iota(I32, (slots, slots), 0)
    across = lax.broadcasted_iota(I32, (slots, slots), 1)
    column = jnp.sum(jnp.where(down == across, owner, 0), axis=1, keepdims=True)
    earlier = (owner == column) & (down < across)
    rank = jnp.sum(earlier.astype(I32), axis=0, keepdims=True)
    return (rows // share_tiles) * per_share + rank


def emissions(scaled, background, ensemble, emis, c):
    blocks = ensemble.shape[2] // 128
    values = background[c] + jnp.dot(scaled, ensemble[c], preferred_element_type=F32)
    for b in range(blocks):
        emis[c * blocks + b] = values[:, b * 128 : (b + 1) * 128]


def live_groups(live, unroll, work):
    lax.fori_loop(0, (live + unroll - 1) // unroll, lambda g, carry: (work(g), carry)[1], 0)


def forward_group(g, unroll, block, place, tiles, hour_rows, emis, partial):
    hours = emis.shape[1]
    hour_line = lax.broadcasted_iota(I32, (hours, 128), 0)
    none = jnp.zeros((hours, 128), F32)
    base = pl.multiple_of(g * unroll, unroll)
    these = hour_rows[pl.ds(base, unroll), :]
    for u in range(0, unroll, 2):
        s = base + u
        left = jnp.concatenate([emis[block[0, s]], none], axis=1)
        right = jnp.concatenate([none, emis[block[0, s + 1]]], axis=1)
        pair = jnp.concatenate([left, right], axis=0).astype(BF16)
        both = jnp.concatenate([tiles[s], tiles[s + 1]], axis=1)
        every = lax.dot_general(pair, both, (((1,), (1,)), ((), ())), preferred_element_type=F32)
        for v in range(2):
            chosen = hour_line == these[u + v : u + v + 1, :]
            part = jnp.where(chosen, every[v * hours : (v + 1) * hours], 0.0)
            partial[pl.ds(place[0, s + v], 1), :] = jnp.sum(part, axis=0, keepdims=True)


def first_forward_kernel(
    count, block_in, row_in, control, background, ensemble, footprint, hour,
    observed, inv_var,
    out, place, block, hour_rows, bg_buf, ens_buf, tile_buf, own_observed, own_inv_var,
    place_buf, row, line_buf, control_buf, hour_buf, emis, partial, row_ids,
    ens_sem, bg_sem, tile_sem, hour_sem, place_sem, small_sem,
):
    slots = tile_buf.shape[0]
    width = ens_buf.shape[2]
    senders = out.shape[0]
    share_tiles = own_observed.shape[0]
    chunks = slots // TILE_CHUNK

    def ens_copy(c):
        return pltpu.make_async_copy(
            ensemble.at[:, pl.ds(c * width, width)], ens_buf.at[c], ens_sem.at[c]
        )

    def bg_copy(c):
        return pltpu.make_async_copy(
            background.at[:, pl.ds(c * width, width)], bg_buf.at[c], bg_sem.at[c]
        )

    def tile_copy(c):
        part = pl.ds(c * TILE_CHUNK, TILE_CHUNK)
        return pltpu.make_async_copy(footprint.at[part], tile_buf.at[part], tile_sem.at[c])

    share = pl.ds(lax.axis_index(CELLS) * share_tiles, share_tiles)
    pairs = [
        (row_in, line_buf), (control, control_buf), (row_in, row),
        (block_in, block), (observed.at[share], own_observed), (inv_var.at[share], own_inv_var),
    ]
    small = [pltpu.make_async_copy(a, b, small_sem.at[i]) for i, (a, b) in enumerate(pairs)]
    for copy in small[:4]:
        copy.start()
    hour_copy = pltpu.make_async_copy(hour, hour_buf, hour_sem)
    for c in range(ENS_CHUNKS):
        ens_copy(c).start()
        bg_copy(c).start()
        if c == HOURS_AFTER:
            hour_copy.start()

    small[0].wait()
    live = count[0, 0]
    places = slot_places(line_buf[...], share_tiles, slots // senders)
    place_buf[...] = jnp.concatenate([places, jnp.full((1, 128), live)], axis=1)
    place_copy = pltpu.make_async_copy(place_buf, place, place_sem)
    place_copy.start()
    partial[...] = jnp.zeros_like(partial)
    row_ids[...] = jnp.zeros_like(row_ids)
    filled = ((live + FIRST_UNROLL - 1) // FIRST_UNROLL) * FIRST_UNROLL
    named = ((live + UNROLL - 1) // UNROLL) * UNROLL
    small[1].wait()
    scaled = control_buf[...].astype(BF16)

    def start_tiles(c):
        @pl.when(c * TILE_CHUNK < filled)
        def _():
            tile_copy(c).start()

    def name_slots(g, carry):
        for u in range(NAMES):
            s = g * NAMES + u
            here = row[0, s]
            shown = hour_buf[pl.ds(here, 1), :]
            hour_rows[pl.ds(s, 1), :] = jnp.where(s < live, shown, -1)
            number = (here & (share_tiles - 1)).astype(F32)
            row_ids[pl.ds(place[0, s], 1), :] = jnp.full((1, 128), number)
        return carry

    for c in range(ENS_CHUNKS):
        ens_copy(c).wait()
        bg_copy(c).wait()
        for t in range(chunks):
            if ENS_CHUNKS - 1 - (chunks - 1 - t) // TILES_AT_ONCE == c:
                start_tiles(t)
        emissions(scaled, bg_buf, ens_buf, emis, c)
        if c == HOURS_AFTER + 2:
            small[2].wait()
            place_copy.wait()
            hour_copy.wait()
            lax.fori_loop(0, named // NAMES, name_slots, 0)
    small[4].start()
    small[5].start()
    small[3].wait()

    def work(g):
        for part in range(FIRST_UNROLL // TILE_CHUNK):
            tile_copy(g * (FIRST_UNROLL // TILE_CHUNK) + part).wait()
        forward_group(g, FIRST_UNROLL, block, place, tile_buf, hour_rows, emis, partial)

    live_groups(live, FIRST_UNROLL, work)
    small[4].wait()
    small[5].wait()
    parts = [part[...].reshape(senders, slots // senders, 128) for part in (partial, row_ids)]
    out[...] = jnp.concatenate(parts, axis=1).astype(BF16)


def next_forward_kernel(
    block, place, control, copies, hour_rows, bg_buf, ens_buf, tile_buf,
    out, gradient, emis, partial,
):
    live = place[0, tile_buf.shape[0]]
    total = control[...] + jnp.sum(copies[...].astype(F32), axis=0)
    gradient[...] = total
    scaled = (control[...] - step_size * total).astype(BF16)
    partial[...] = jnp.zeros_like(partial)
    for c in range(ENS_CHUNKS):
        emissions(scaled, bg_buf, ens_buf, emis, c)
    live_groups(
        live, UNROLL,
        lambda g: forward_group(g, UNROLL, block, place, tile_buf, hour_rows, emis, partial),
    )
    out[...] = partial[...].astype(BF16)


def owner_pick(received, tiles):
    ids = received[...].astype(F32)[:, 8:16, 0:tiles].reshape(received.shape[0] * 8, tiles)
    lane = lax.broadcasted_iota(I32, ids.shape, 1).astype(F32)
    return jnp.where(ids == lane, 1.0, 0.0).astype(BF16)


def own_sum(pick, received):
    return lax.dot_general(pick, received, (((0,), (0,)), ((), ())), preferred_element_type=F32)


def send_departure(pick, own, observed, inv_var, send):
    departure = (inv_var[...] * (own - observed[...])).astype(BF16)
    send[...] = jnp.dot(pick, departure, preferred_element_type=F32).astype(BF16)


def first_departure_kernel(received, observed, inv_var, send):
    pick = owner_pick(received, observed.shape[0])
    data = received[...].astype(F32)[:, 0:8, :].reshape(pick.shape[0], 128).astype(BF16)
    send_departure(pick, own_sum(pick, data), observed, inv_var, send)


def next_departure_kernel(named, received, observed, inv_var, modelled, send):
    pick = owner_pick(named, observed.shape[0])
    own = own_sum(pick, received[...])
    modelled[...] = own
    send_departure(pick, own, observed, inv_var, send)


def adjoint_kernel(
    block, place, departures, hour_rows, ens_buf, tile_buf, out, dep_buf, adjoint
):
    hours = out.shape[1]
    blocks = ens_buf.shape[2] // 128
    live = place[0, tile_buf.shape[0]]
    hour_line = lax.broadcasted_iota(I32, (hours, 128), 0)
    dep_buf[...] = departures[...].astype(F32)
    adjoint[...] = jnp.zeros_like(adjoint)

    def work(g):
        base = pl.multiple_of(g * UNROLL, UNROLL)
        these = hour_rows[pl.ds(base, UNROLL), :]
        for u in range(0, UNROLL, 2):
            s = base + u
            weighted = []
            for v in range(2):
                chosen = hour_line == these[u + v : u + v + 1, :]
                weighted.append(jnp.where(chosen, dep_buf[pl.ds(place[0, s + v], 1), :], 0.0))
            pair = jnp.concatenate(weighted, axis=0).astype(BF16)
            loaded = jnp.minimum(s, live - 1)
            beside = jnp.minimum(s + 1, live - 1)
            both = jnp.concatenate([tile_buf[loaded], tile_buf[beside]], axis=1)
            every = jnp.dot(pair, both, preferred_element_type=F32)
            adjoint[block[0, s]] += every[0:hours, 0:128]
            adjoint[block[0, s + 1]] += every[hours : 2 * hours, 128:256]

    live_groups(live, UNROLL, work)
    total = jnp.zeros((ens_buf.shape[1], hours), F32)
    for c in range(ENS_CHUNKS):
        rounded = jnp.concatenate([adjoint[c * blocks + b] for b in range(blocks)], axis=1)
        total = total + lax.dot_general(
            ens_buf[c], rounded.astype(BF16), (((1,), (1,)), ((), ())), preferred_element_type=F32
        )
    total = jnp.transpose(total)
    total = total.astype(BF16)
    for j in range(out.shape[0]):
        out[j] = total


def last_adjoint_kernel(
    block, place, departures, hour_rows, ens_buf, tile_buf, own, out, final,
    dep_buf, adjoint, sem,
):
    copy = pltpu.make_async_copy(own, final, sem)
    copy.start()
    adjoint_kernel(
        block, place, departures, hour_rows, ens_buf, tile_buf, out, dep_buf, adjoint
    )
    copy.wait()


def sum_kernel(copies, out):
    total = jnp.sum(copies[...].astype(F32), axis=0).astype(out.dtype)
    for j in range(out.shape[0]):
        out[j] = total


def exchange(value, axes):
    return lax.all_to_all(value, axes, 0, 0, tiled=True)


def per_device(
    control, background, ensemble, footprint, tile_block, tile_row, tile_count, hour, observed, inv_var,
):
    hours, members = control.shape
    cells_dev = background.shape[1]
    slots = footprint.shape[1]
    receptors = hour.shape[1]
    row_tiles = receptors // 128
    devices = lax.axis_size(CELLS)
    plane = lax.axis_size(PLANE)
    rest = lax.axis_size(REST)
    share_tiles = row_tiles // devices
    width = cells_dev // ENS_CHUNKS

    hour_tab = hour.reshape(row_tiles, 128)
    obs_tab = observed.reshape(row_tiles, 128)
    var_tab = inv_var.reshape(row_tiles, 128)

    smem = pl.BlockSpec(memory_space=pltpu.SMEM)
    vmem = pl.BlockSpec(memory_space=pltpu.VMEM)
    hbm = pl.BlockSpec(memory_space=pl.ANY)
    limit = pltpu.CompilerParams(vmem_limit_bytes=24 * 1024 * 1024)
    emis = pltpu.VMEM((cells_dev // 128, hours, 128), F32)
    slot_lines = pltpu.VMEM((slots, 128), F32)

    first_forward = pl.pallas_call(
        first_forward_kernel,
        out_shape=(
            pltpu.VMEM((devices, 16, 128), BF16),
            pltpu.SMEM((1, slots + 128), I32),
            pltpu.SMEM((1, slots), I32),
            pltpu.VMEM((slots, 128), I32),
            pltpu.VMEM((ENS_CHUNKS, hours, width), F32),
            pltpu.VMEM((ENS_CHUNKS, members, width), BF16),
            pltpu.VMEM((slots, 128, 128), BF16),
            pltpu.VMEM((share_tiles, 128), F32),
            pltpu.VMEM((share_tiles, 128), F32),
        ),
        in_specs=[smem] + [hbm] * 9,
        out_specs=(vmem, smem, smem) + (vmem,) * 6,
        scratch_shapes=[
            pltpu.VMEM((1, slots + 128), I32),
            pltpu.SMEM((1, slots), I32),
            pltpu.VMEM((1, slots), I32),
            pltpu.VMEM((hours, members), F32),
            pltpu.VMEM((row_tiles, 128), I32),
            emis,
            slot_lines,
            slot_lines,
            pltpu.SemaphoreType.DMA((ENS_CHUNKS,)),
            pltpu.SemaphoreType.DMA((ENS_CHUNKS,)),
            pltpu.SemaphoreType.DMA((slots // TILE_CHUNK,)),
            pltpu.SemaphoreType.DMA,
            pltpu.SemaphoreType.DMA,
            pltpu.SemaphoreType.DMA((6,)),
        ],
        compiler_params=limit,
        name="first_forward",
    )
    next_forward = pl.pallas_call(
        next_forward_kernel,
        out_shape=(
            pltpu.VMEM((slots, 128), BF16),
            jax.ShapeDtypeStruct((hours, members), F32),
        ),
        in_specs=[smem, smem] + [vmem] * 6,
        out_specs=(vmem, vmem),
        scratch_shapes=[emis, slot_lines],
        compiler_params=limit,
        name="next_forward",
    )

    sent = pltpu.VMEM((slots, 128), BF16)
    own = pltpu.VMEM((share_tiles, 128), F32)

    def depart(kernel, arrays, out_shape, name):
        return pl.pallas_call(
            kernel,
            out_shape=out_shape,
            in_specs=[vmem] * arrays,
            out_specs=(vmem,) * len(out_shape),
            compiler_params=pltpu.CompilerParams(vmem_limit_bytes=4 * 1024 * 1024),
            name=name,
        )

    adjoint = pl.pallas_call(
        adjoint_kernel,
        out_shape=pltpu.VMEM((plane, hours, members), BF16),
        in_specs=[smem, smem] + [vmem] * 4,
        out_specs=vmem,
        scratch_shapes=[slot_lines, emis],
        compiler_params=limit,
        name="adjoint",
    )

    def add_copies(copies, count, kind):
        return pl.pallas_call(
            sum_kernel,
            out_shape=pltpu.VMEM((count, hours, members), kind),
            in_specs=[vmem],
            out_specs=vmem,
            compiler_params=pltpu.CompilerParams(vmem_limit_bytes=4 * 1024 * 1024),
            name="add_copies",
        )(copies)

    last_adjoint = pl.pallas_call(
        last_adjoint_kernel,
        out_shape=(
            pltpu.VMEM((rest, hours, members), BF16),
            jax.ShapeDtypeStruct((share_tiles, 128), F32),
        ),
        in_specs=[smem, smem] + [vmem] * 5,
        out_specs=(vmem, hbm),
        scratch_shapes=[slot_lines, emis, pltpu.SemaphoreType.DMA],
        compiler_params=limit,
        name="last_adjoint",
    )

    def by_slots(rows):
        return exchange(rows.reshape(devices, slots // devices, 128), CELLS).reshape(slots, 128)

    pinned = [
        pltpu.with_memory_space_constraint(array, pltpu.HBM)
        for array in (
            tile_block, tile_row, control, background, ensemble, footprint[0],
            hour_tab, obs_tab, var_tab,
        )
    ]
    partials, place, block, hour_rows, bg_buf, ens_buf, tile_buf, own_obs, own_var = first_forward(
        tile_count, *pinned
    )
    named = exchange(partials, CELLS)
    (send,) = depart(first_departure_kernel, 3, (sent,), "first_departure")(named, own_obs, own_var)
    kept = (hour_rows, ens_buf, tile_buf)
    copies = adjoint(block, place, by_slots(send), *kept)
    copies = exchange(add_copies(exchange(copies, PLANE), rest, F32), REST)
    partials, first_grad = next_forward(
        block, place, control, copies, hour_rows, bg_buf, ens_buf, tile_buf
    )
    received = by_slots(partials)
    modelled, send = depart(next_departure_kernel, 4, (own, sent), "next_departure")(
        named, received, own_obs, own_var
    )
    copies, final = last_adjoint(
        block, place, by_slots(send), *kept, modelled
    )
    copies = exchange(add_copies(exchange(copies, REST), plane, BF16), PLANE)
    updated = control - step_size * first_grad
    second_grad = updated + jnp.sum(copies.astype(F32), axis=0)
    return jnp.stack([first_grad, second_grad]), final.reshape(1, receptors // devices)


def solution(mesh):
    torus = Mesh(
        mesh.devices.reshape(4, 4, 2, mesh.shape["rcpt"]), ("cells_0", "cells_1", "cells_2", "rcpt")
    )
    return jax.shard_map(
        per_device,
        mesh=torus,
        in_specs=(
            P(),
            P(None, CELLS),
            P(None, CELLS),
            P("rcpt", CELLS, None, None),
            P("rcpt", CELLS),
            P("rcpt", CELLS),
            P("rcpt", CELLS),
            P("rcpt", None),
            P("rcpt", None),
            P("rcpt", None),
        ),
        out_specs=(P(), P("rcpt", CELLS)),
        check_vma=False,
    )
```

```python
import jax
import jax.numpy as jnp
from jax import lax
from jax.experimental import pallas as pl
from jax.experimental.pallas import tpu as pltpu
from jax.sharding import Mesh
from jax.sharding import PartitionSpec as P

CELLS = ("cells_0", "cells_1", "cells_2")
PLANE = ("cells_0", "cells_1")
REST = ("cells_2", "rcpt")

step_size = 0.5

ENS_CHUNKS = 16
HOURS_AFTER = 5
TILES_AT_ONCE = 1
TILE_CHUNK = 32
FIRST_UNROLL = 64
UNROLL = 128
NAMES = 8
F32 = jnp.float32
BF16 = jnp.bfloat16
I32 = jnp.int32


def slot_places(rows, share_tiles, per_share):
    slots = rows.shape[1]
    owner = jnp.broadcast_to(rows // share_tiles, (slots, slots))
    down = lax.broadcasted_iota(I32, (slots, slots), 0)
    across = lax.broadcasted_iota(I32, (slots, slots), 1)
    column = jnp.sum(jnp.where(down == across, owner, 0), axis=1, keepdims=True)
    earlier = (owner == column) & (down < across)
    rank = jnp.sum(earlier.astype(I32), axis=0, keepdims=True)
    return (rows // share_tiles) * per_share + rank


def emissions(scaled, background, ensemble, emis, c):
    blocks = ensemble.shape[2] // 128
    values = background[c] + jnp.dot(scaled, ensemble[c], preferred_element_type=F32)
    for b in range(blocks):
        emis[c * blocks + b] = values[:, b * 128 : (b + 1) * 128]


def live_groups(live, unroll, work):
    lax.fori_loop(0, (live + unroll - 1) // unroll, lambda g, carry: (work(g), carry)[1], 0)


def forward_group(g, unroll, block, place, tiles, hour_rows, emis, partial):
    hours = emis.shape[1]
    hour_line = lax.broadcasted_iota(I32, (hours, 128), 0)
    none = jnp.zeros((hours, 128), F32)
    base = pl.multiple_of(g * unroll, unroll)
    these = hour_rows[pl.ds(base, unroll), :]
    for u in range(0, unroll, 2):
        s = base + u
        left = jnp.concatenate([emis[block[0, s]], none], axis=1)
        right = jnp.concatenate([none, emis[block[0, s + 1]]], axis=1)
        pair = jnp.concatenate([left, right], axis=0).astype(BF16)
        both = jnp.concatenate([tiles[s], tiles[s + 1]], axis=1)
        every = lax.dot_general(pair, both, (((1,), (1,)), ((), ())), preferred_element_type=F32)
        for v in range(2):
            chosen = hour_line == these[u + v : u + v + 1, :]
            part = jnp.where(chosen, every[v * hours : (v + 1) * hours], 0.0)
            partial[pl.ds(place[0, s + v], 1), :] = jnp.sum(part, axis=0, keepdims=True)


def first_forward_kernel(
    count, block_in, row_in, control, background, ensemble, footprint, hour,
    observed, inv_var,
    out, place, block, hour_rows, bg_buf, ens_buf, tile_buf, own_observed, own_inv_var,
    place_buf, row, line_buf, control_buf, hour_buf, emis, partial, row_ids,
    ens_sem, bg_sem, tile_sem, hour_sem, place_sem, small_sem,
):
    slots = tile_buf.shape[0]
    width = ens_buf.shape[2]
    senders = out.shape[0]
    share_tiles = own_observed.shape[0]
    chunks = slots // TILE_CHUNK

    def ens_copy(c):
        return pltpu.make_async_copy(
            ensemble.at[:, pl.ds(c * width, width)], ens_buf.at[c], ens_sem.at[c]
        )

    def bg_copy(c):
        return pltpu.make_async_copy(
            background.at[:, pl.ds(c * width, width)], bg_buf.at[c], bg_sem.at[c]
        )

    def tile_copy(c):
        part = pl.ds(c * TILE_CHUNK, TILE_CHUNK)
        return pltpu.make_async_copy(footprint.at[part], tile_buf.at[part], tile_sem.at[c])

    share = pl.ds(lax.axis_index(CELLS) * share_tiles, share_tiles)
    pairs = [
        (row_in, line_buf), (control, control_buf), (row_in, row),
        (block_in, block), (observed.at[share], own_observed), (inv_var.at[share], own_inv_var),
    ]
    small = [pltpu.make_async_copy(a, b, small_sem.at[i]) for i, (a, b) in enumerate(pairs)]
    for copy in small[:4]:
        copy.start()
    hour_copy = pltpu.make_async_copy(hour, hour_buf, hour_sem)
    for c in range(ENS_CHUNKS):
        ens_copy(c).start()
        bg_copy(c).start()
        if c == HOURS_AFTER:
            hour_copy.start()

    small[0].wait()
    live = count[0, 0]
    places = slot_places(line_buf[...], share_tiles, slots // senders)
    place_buf[...] = jnp.concatenate([places, jnp.full((1, 128), live)], axis=1)
    place_copy = pltpu.make_async_copy(place_buf, place, place_sem)
    place_copy.start()
    partial[...] = jnp.zeros_like(partial)
    row_ids[...] = jnp.zeros_like(row_ids)
    filled = ((live + FIRST_UNROLL - 1) // FIRST_UNROLL) * FIRST_UNROLL
    named = ((live + UNROLL - 1) // UNROLL) * UNROLL
    small[1].wait()
    scaled = control_buf[...].astype(BF16)

    def start_tiles(c):
        @pl.when(c * TILE_CHUNK < filled)
        def _():
            tile_copy(c).start()

    def name_slots(g, carry):
        for u in range(NAMES):
            s = g * NAMES + u
            here = row[0, s]
            shown = hour_buf[pl.ds(here, 1), :]
            hour_rows[pl.ds(s, 1), :] = jnp.where(s < live, shown, -1)
            number = (here & (share_tiles - 1)).astype(F32)
            row_ids[pl.ds(place[0, s], 1), :] = jnp.full((1, 128), number)
        return carry

    for c in range(ENS_CHUNKS):
        ens_copy(c).wait()
        bg_copy(c).wait()
        for t in range(chunks):
            if ENS_CHUNKS - 1 - (chunks - 1 - t) // TILES_AT_ONCE == c:
                start_tiles(t)
        emissions(scaled, bg_buf, ens_buf, emis, c)
        if c == HOURS_AFTER + 2:
            small[2].wait()
            place_copy.wait()
            hour_copy.wait()
            lax.fori_loop(0, named // NAMES, name_slots, 0)
    small[4].start()
    small[5].start()
    small[3].wait()

    def work(g):
        for part in range(FIRST_UNROLL // TILE_CHUNK):
            tile_copy(g * (FIRST_UNROLL // TILE_CHUNK) + part).wait()
        forward_group(g, FIRST_UNROLL, block, place, tile_buf, hour_rows, emis, partial)

    live_groups(live, FIRST_UNROLL, work)
    small[4].wait()
    small[5].wait()
    parts = [part[...].reshape(senders, slots // senders, 128) for part in (partial, row_ids)]
    out[...] = jnp.concatenate(parts, axis=1).astype(BF16)


def next_forward_kernel(
    block, place, control, copies, hour_rows, bg_buf, ens_buf, tile_buf,
    out, gradient, emis, partial,
):
    live = place[0, tile_buf.shape[0]]
    total = control[...] + jnp.sum(copies[...].astype(F32), axis=0)
    gradient[...] = total
    scaled = (control[...] - step_size * total).astype(BF16)
    partial[...] = jnp.zeros_like(partial)
    for c in range(ENS_CHUNKS):
        emissions(scaled, bg_buf, ens_buf, emis, c)
    live_groups(
        live, UNROLL,
        lambda g: forward_group(g, UNROLL, block, place, tile_buf, hour_rows, emis, partial),
    )
    out[...] = partial[...].astype(BF16)


def owner_pick(received, tiles):
    ids = received[...].astype(F32)[:, 8:16, 0:tiles].reshape(received.shape[0] * 8, tiles)
    lane = lax.broadcasted_iota(I32, ids.shape, 1).astype(F32)
    return jnp.where(ids == lane, 1.0, 0.0).astype(BF16)


def own_sum(pick, received):
    return lax.dot_general(pick, received, (((0,), (0,)), ((), ())), preferred_element_type=F32)


def send_departure(pick, own, observed, inv_var, send):
    departure = (inv_var[...] * (own - observed[...])).astype(BF16)
    send[...] = jnp.dot(pick, departure, preferred_element_type=F32).astype(BF16)


def first_departure_kernel(received, observed, inv_var, send):
    pick = owner_pick(received, observed.shape[0])
    data = received[...].astype(F32)[:, 0:8, :].reshape(pick.shape[0], 128).astype(BF16)
    send_departure(pick, own_sum(pick, data), observed, inv_var, send)


def next_departure_kernel(named, received, observed, inv_var, modelled, send):
    pick = owner_pick(named, observed.shape[0])
    own = own_sum(pick, received[...])
    modelled[...] = own
    send_departure(pick, own, observed, inv_var, send)


def adjoint_kernel(
    block, place, departures, hour_rows, ens_buf, tile_buf, out, dep_buf, adjoint
):
    hours = out.shape[1]
    blocks = ens_buf.shape[2] // 128
    live = place[0, tile_buf.shape[0]]
    hour_line = lax.broadcasted_iota(I32, (hours, 128), 0)
    dep_buf[...] = departures[...].astype(F32)
    adjoint[...] = jnp.zeros_like(adjoint)

    def work(g):
        base = pl.multiple_of(g * UNROLL, UNROLL)
        these = hour_rows[pl.ds(base, UNROLL), :]
        for u in range(0, UNROLL, 2):
            s = base + u
            weighted = []
            for v in range(2):
                chosen = hour_line == these[u + v : u + v + 1, :]
                weighted.append(jnp.where(chosen, dep_buf[pl.ds(place[0, s + v], 1), :], 0.0))
            pair = jnp.concatenate(weighted, axis=0).astype(BF16)
            loaded = jnp.minimum(s, live - 1)
            beside = jnp.minimum(s + 1, live - 1)
            both = jnp.concatenate([tile_buf[loaded], tile_buf[beside]], axis=1)
            every = jnp.dot(pair, both, preferred_element_type=F32)
            adjoint[block[0, s]] += every[0:hours, 0:128]
            adjoint[block[0, s + 1]] += every[hours : 2 * hours, 128:256]

    live_groups(live, UNROLL, work)
    total = jnp.zeros((ens_buf.shape[1], hours), F32)
    for c in range(ENS_CHUNKS):
        rounded = jnp.concatenate([adjoint[c * blocks + b] for b in range(blocks)], axis=1)
        total = total + lax.dot_general(
            ens_buf[c], rounded.astype(BF16), (((1,), (1,)), ((), ())), preferred_element_type=F32
        )
    total = jnp.transpose(total)
    total = total.astype(BF16)
    for j in range(out.shape[0]):
        out[j] = total


def last_adjoint_kernel(
    block, place, departures, hour_rows, ens_buf, tile_buf, own, out, final,
    dep_buf, adjoint, sem,
):
    copy = pltpu.make_async_copy(own, final, sem)
    copy.start()
    adjoint_kernel(
        block, place, departures, hour_rows, ens_buf, tile_buf, out, dep_buf, adjoint
    )
    copy.wait()


def sum_kernel(copies, out):
    total = jnp.sum(copies[...].astype(F32), axis=0).astype(out.dtype)
    for j in range(out.shape[0]):
        out[j] = total


def exchange(value, axes):
    return lax.all_to_all(value, axes, 0, 0, tiled=True)


def per_device(
    control, background, ensemble, footprint, tile_block, tile_row, tile_count, hour, observed, inv_var,
):
    hours, members = control.shape
    cells_dev = background.shape[1]
    slots = footprint.shape[1]
    receptors = hour.shape[1]
    row_tiles = receptors // 128
    devices = lax.axis_size(CELLS)
    plane = lax.axis_size(PLANE)
    rest = lax.axis_size(REST)
    share_tiles = row_tiles // devices
    width = cells_dev // ENS_CHUNKS

    hour_tab = hour.reshape(row_tiles, 128)
    obs_tab = observed.reshape(row_tiles, 128)
    var_tab = inv_var.reshape(row_tiles, 128)

    smem = pl.BlockSpec(memory_space=pltpu.SMEM)
    vmem = pl.BlockSpec(memory_space=pltpu.VMEM)
    hbm = pl.BlockSpec(memory_space=pl.ANY)
    limit = pltpu.CompilerParams(vmem_limit_bytes=24 * 1024 * 1024)
    emis = pltpu.VMEM((cells_dev // 128, hours, 128), F32)
    slot_lines = pltpu.VMEM((slots, 128), F32)

    first_forward = pl.pallas_call(
        first_forward_kernel,
        out_shape=(
            pltpu.VMEM((devices, 16, 128), BF16),
            pltpu.SMEM((1, slots + 128), I32),
            pltpu.SMEM((1, slots), I32),
            pltpu.VMEM((slots, 128), I32),
            pltpu.VMEM((ENS_CHUNKS, hours, width), F32),
            pltpu.VMEM((ENS_CHUNKS, members, width), BF16),
            pltpu.VMEM((slots, 128, 128), BF16),
            pltpu.VMEM((share_tiles, 128), F32),
            pltpu.VMEM((share_tiles, 128), F32),
        ),
        in_specs=[smem] + [hbm] * 9,
        out_specs=(vmem, smem, smem) + (vmem,) * 6,
        scratch_shapes=[
            pltpu.VMEM((1, slots + 128), I32),
            pltpu.SMEM((1, slots), I32),
            pltpu.VMEM((1, slots), I32),
            pltpu.VMEM((hours, members), F32),
            pltpu.VMEM((row_tiles, 128), I32),
            emis,
            slot_lines,
            slot_lines,
            pltpu.SemaphoreType.DMA((ENS_CHUNKS,)),
            pltpu.SemaphoreType.DMA((ENS_CHUNKS,)),
            pltpu.SemaphoreType.DMA((slots // TILE_CHUNK,)),
            pltpu.SemaphoreType.DMA,
            pltpu.SemaphoreType.DMA,
            pltpu.SemaphoreType.DMA((6,)),
        ],
        compiler_params=limit,
        name="first_forward",
    )
    next_forward = pl.pallas_call(
        next_forward_kernel,
        out_shape=(
            pltpu.VMEM((slots, 128), BF16),
            jax.ShapeDtypeStruct((hours, members), F32),
        ),
        in_specs=[smem, smem] + [vmem] * 6,
        out_specs=(vmem, vmem),
        scratch_shapes=[emis, slot_lines],
        compiler_params=limit,
        name="next_forward",
    )

    sent = pltpu.VMEM((slots, 128), BF16)
    own = pltpu.VMEM((share_tiles, 128), F32)

    def depart(kernel, arrays, out_shape, name):
        return pl.pallas_call(
            kernel,
            out_shape=out_shape,
            in_specs=[vmem] * arrays,
            out_specs=(vmem,) * len(out_shape),
            compiler_params=pltpu.CompilerParams(vmem_limit_bytes=4 * 1024 * 1024),
            name=name,
        )

    adjoint = pl.pallas_call(
        adjoint_kernel,
        out_shape=pltpu.VMEM((plane, hours, members), BF16),
        in_specs=[smem, smem] + [vmem] * 4,
        out_specs=vmem,
        scratch_shapes=[slot_lines, emis],
        compiler_params=limit,
        name="adjoint",
    )

    def add_copies(copies, count, kind):
        return pl.pallas_call(
            sum_kernel,
            out_shape=pltpu.VMEM((count, hours, members), kind),
            in_specs=[vmem],
            out_specs=vmem,
            compiler_params=pltpu.CompilerParams(vmem_limit_bytes=4 * 1024 * 1024),
            name="add_copies",
        )(copies)

    last_adjoint = pl.pallas_call(
        last_adjoint_kernel,
        out_shape=(
            pltpu.VMEM((rest, hours, members), BF16),
            jax.ShapeDtypeStruct((share_tiles, 128), F32),
        ),
        in_specs=[smem, smem] + [vmem] * 5,
        out_specs=(vmem, hbm),
        scratch_shapes=[slot_lines, emis, pltpu.SemaphoreType.DMA],
        compiler_params=limit,
        name="last_adjoint",
    )

    def by_slots(rows):
        return exchange(rows.reshape(devices, slots // devices, 128), CELLS).reshape(slots, 128)

    pinned = [
        pltpu.with_memory_space_constraint(array, pltpu.HBM)
        for array in (
            tile_block, tile_row, control, background, ensemble, footprint[0],
            hour_tab, obs_tab, var_tab,
        )
    ]
    partials, place, block, hour_rows, bg_buf, ens_buf, tile_buf, own_obs, own_var = first_forward(
        tile_count, *pinned
    )
    named = exchange(partials, CELLS)
    (send,) = depart(first_departure_kernel, 3, (sent,), "first_departure")(named, own_obs, own_var)
    kept = (hour_rows, ens_buf, tile_buf)
    copies = adjoint(block, place, by_slots(send), *kept)
    copies = exchange(add_copies(exchange(copies, PLANE), rest, F32), REST)
    partials, first_grad = next_forward(
        block, place, control, copies, hour_rows, bg_buf, ens_buf, tile_buf
    )
    received = by_slots(partials)
    modelled, send = depart(next_departure_kernel, 4, (own, sent), "next_departure")(
        named, received, own_obs, own_var
    )
    copies, final = last_adjoint(
        block, place, by_slots(send), *kept, modelled
    )
    copies = exchange(add_copies(exchange(copies, REST), plane, BF16), PLANE)
    updated = control - step_size * first_grad
    second_grad = updated + jnp.sum(copies.astype(F32), axis=0)
    return jnp.stack([first_grad, second_grad]), final.reshape(1, receptors // devices)


def solution(mesh):
    torus = Mesh(
        mesh.devices.reshape(4, 4, 2, mesh.shape["rcpt"]), ("cells_0", "cells_1", "cells_2", "rcpt")
    )
    return jax.shard_map(
        per_device,
        mesh=torus,
        in_specs=(
            P(),
            P(None, CELLS),
            P(None, CELLS),
            P("rcpt", CELLS, None, None),
            P("rcpt", CELLS),
            P("rcpt", CELLS),
            P("rcpt", CELLS),
            P("rcpt", None),
            P("rcpt", None),
            P("rcpt", None),
        ),
        out_specs=(P(), P("rcpt", CELLS)),
        check_vma=False,
    )
```
